32 devices in a mesh: kv: 4 (over y, x), seq: 8 (over z, core).
Axes of the slice: x: 2, y: 2, z: 4, core: 2. Of those that a mesh axis runs over, the one named last changes fastest.
Arguments:
- queries: bfloat16 [1024, 12288], P('seq', 'kv'), may hold values from -400 to 400
- cache_keys: bfloat16 [8192, 768], P('seq', 'kv'), may hold values from -6 to 6
- cache_values: bfloat16 [8192, 512], P('seq', 'kv'), may hold values from -6 to 6
- incoming_keys: bfloat16 [1024, 768], P('seq', 'kv'), may hold values from -6 to 6
- new_values: bfloat16 [1024, 512], P('seq', 'kv'), may hold values from -6 to 6
- comp_key_weight: bfloat16 [6144, 192], P('kv'), may hold values from -0.078125 to 0.078125
- comp_value_weight: bfloat16 [4096, 128], P('kv'), may hold values from -0.09375 to 0.09375
- select_blocks: int32 [32, 4, 16], P('seq', 'kv'), may hold values from 0 to 127, as said below
- gate_weight: bfloat16 [64, 192, 3], P('kv'), may hold values from -0.4375 to 0.4375
Outputs:
- attended: bfloat16 [1024, 8192], P('seq', 'kv')
The draws below stay inside these ranges and needn't reach their ends.
Inputs may be any that keep to these rules, and one draw needn't show every extreme that they name: `select_blocks`: each row names 16 different blocks. For each KV group, the rows of one device of seq (4 tiles) name blocks of any one cache shard (the 16 blocks of one index of seq) at most 16 times in all, and in every draw the rows of every device name one shard's blocks exactly 16 times.
All inputs are finite; a program needn't handle non-finite values.
Results may differ from the reference program's by a relative error of at most 0.012.
Values may be sent and summed in bfloat16 or wider, within the bound.
A program may use at most 128 MiB of HBM per device.

```python
import jax
import jax.numpy as jnp
from jax import lax

HEADS = 64
KV_GROUPS = 4
HEAD_QK = 192
HEAD_V = 128
CMP_STRIDE = 16
SEL_BLOCK = 64
TOPN = 16
WINDOW = 512
TILE = 32
Q_DEV = 128
QUERIES = 1024
CACHE = 8192
TILES_DEV = 4
BLK_DEV = 16
CAP = 16
N_SEQ = 8


def draw_queries(key, part):
    drawn = jax.random.normal(jax.random.fold_in(key, 11), (QUERIES, HEADS * HEAD_QK), jnp.float32) * 2.5
    return jnp.clip(drawn, -400.0, 400.0).astype(jnp.bfloat16)


def one_device(subkey, busy):
    picks = TILES_DEV * TOPN
    slots = N_SEQ * CAP
    key_score, key_offset, key_order = jax.random.split(subkey, 3)
    places = jnp.arange(slots, dtype=jnp.int32)
    pool = places // CAP
    score = jax.random.randint(key_score, (slots,), 0, 1 << 16, dtype=jnp.int32) * slots + places
    score = jnp.where(pool == busy, places - slots, score)
    owner = pool[jnp.argsort(score, stable=True)][:picks]
    owner = owner[jax.random.permutation(key_order, picks)].reshape(TILES_DEV, TOPN)
    onehot = (owner[:, :, None] == jnp.arange(N_SEQ, dtype=jnp.int32)[None, None, :]).astype(jnp.int32)
    ranking = jnp.sum((jnp.cumsum(onehot, axis=1) - 1) * onehot, axis=2)
    offset = jax.random.randint(key_offset, (TILES_DEV, N_SEQ), 0, BLK_DEV, dtype=jnp.int32)
    local = (jnp.take_along_axis(offset, owner, axis=1) + ranking) % BLK_DEV
    return owner * BLK_DEV + local


def draw_select_blocks(key, part):
    columns = []
    for group in range(KV_GROUPS):
        group_key = jax.random.fold_in(key, 101 + group)
        busy = jax.random.randint(jax.random.fold_in(group_key, 7), (), 0, N_SEQ, dtype=jnp.int32)
        subkeys = jax.random.split(jax.random.fold_in(group_key, 9), N_SEQ)
        chosen = jax.vmap(lambda subkey: one_device(subkey, busy))(subkeys)
        columns.append(chosen.reshape(N_SEQ * TILES_DEV, TOPN))
    return jnp.stack(columns, axis=1).astype(jnp.int32)


def shard_levels(key, extent, cuts, least, top_value):
    def one(dim, shards_of):
        heights = jax.random.uniform(jax.random.fold_in(jax.random.fold_in(key, 6), dim), (shards_of,), jnp.float32, least / len(cuts), top_value / len(cuts))
        return jnp.repeat(jnp.exp(heights), extent[dim] // shards_of).reshape((-1,) + (1,) * (len(extent) - dim - 1))

    level = one(*cuts[0])
    for cut in cuts[1:]:
        level = level * one(*cut)
    return level


def normal_values(rng, dims, scale, limit, cuts=(), kind=jnp.bfloat16):
    gain = shard_levels(rng, dims, cuts, -0.22, 0.18) if cuts else 1.0
    result = jax.random.normal(rng, dims, jnp.float32) * scale * gain
    return jnp.minimum(jnp.maximum(result, -limit), limit).astype(kind)


def setup_inputs(seed: int = 0) -> dict:
    key_list = jax.random.split(jax.random.key(seed), 10)
    queries = draw_queries(jax.random.fold_in(key_list[9], 71), 0)
    cache_keys = normal_values(key_list[1], (CACHE, KV_GROUPS * HEAD_QK), 1.0, 6.0, ((0, 8), (1, 4)))
    cache_values = normal_values(key_list[2], (CACHE, KV_GROUPS * HEAD_V), 1.0, 6.0, ((0, 8), (1, 4)))
    incoming_keys = normal_values(key_list[3], (QUERIES, KV_GROUPS * HEAD_QK), 1.0, 6.0, ((0, 8), (1, 4)))
    new_values = normal_values(key_list[4], (QUERIES, KV_GROUPS * HEAD_V), 1.0, 6.0, ((0, 8), (1, 4)))
    comp_key_weight = normal_values(key_list[5], (2 * CMP_STRIDE * HEAD_QK, HEAD_QK), (2 * CMP_STRIDE * HEAD_QK) ** -0.5, 0.078125, ((0, 4),))
    comp_value_weight = normal_values(key_list[6], (2 * CMP_STRIDE * HEAD_V, HEAD_V), (2 * CMP_STRIDE * HEAD_V) ** -0.5, 0.09375, ((0, 4),))
    select_blocks = draw_select_blocks(jax.random.fold_in(key_list[9], 71), 0)
    gate_weight = normal_values(key_list[8], (HEADS, HEAD_QK, 3), HEAD_QK ** -0.5, 0.4375, ((0, 4),))
    return {"queries": queries, "cache_keys": cache_keys, "cache_values": cache_values, "incoming_keys": incoming_keys, "new_values": new_values, "comp_key_weight": comp_key_weight, "comp_value_weight": comp_value_weight, "select_blocks": select_blocks, "gate_weight": gate_weight}


MASKED = -1e30


def attend(rows, keys, values, allowed):
    scale = keys.shape[-1] ** -0.5
    scores = jnp.dot(rows, keys.T, preferred_element_type=jnp.float32) * scale
    scores = jnp.where(allowed, scores, MASKED)
    top = jnp.max(scores, axis=-1, keepdims=True)
    weights = jnp.exp(scores - top)
    total = jnp.sum(weights, axis=-1, keepdims=True)
    mixed = jnp.dot(weights.astype(jnp.bfloat16), values, preferred_element_type=jnp.float32)
    return mixed / total


def reference(queries, cache_keys, cache_values, incoming_keys, new_values, comp_key_weight, comp_value_weight, select_blocks, gate_weight):
    per_group = HEADS // KV_GROUPS
    count = CACHE // CMP_STRIDE - 1
    half_keys = CMP_STRIDE * HEAD_QK
    half_values = CMP_STRIDE * HEAD_V
    split_queries = queries.reshape(QUERIES, KV_GROUPS, per_group, HEAD_QK)
    span = Q_DEV + WINDOW
    offsets = jnp.arange(span, dtype=jnp.int32)[None, :] - jnp.arange(Q_DEV, dtype=jnp.int32)[:, None]
    near_rows = jnp.repeat((offsets > 0) & (offsets <= WINDOW), per_group, axis=0)
    results = []
    for group in range(KV_GROUPS):
        keys = cache_keys[:, group * HEAD_QK:(group + 1) * HEAD_QK]
        values = cache_values[:, group * HEAD_V:(group + 1) * HEAD_V]
        fresh_keys = incoming_keys[:, group * HEAD_QK:(group + 1) * HEAD_QK]
        fresh_values = new_values[:, group * HEAD_V:(group + 1) * HEAD_V]
        comp_keys = (jnp.dot(keys[:CACHE - CMP_STRIDE].reshape(count, half_keys), comp_key_weight[:half_keys], preferred_element_type=jnp.float32)
                     + jnp.dot(keys[CMP_STRIDE:].reshape(count, half_keys), comp_key_weight[half_keys:], preferred_element_type=jnp.float32)).astype(jnp.bfloat16)
        comp_values = (jnp.dot(values[:CACHE - CMP_STRIDE].reshape(count, half_values), comp_value_weight[:half_values], preferred_element_type=jnp.float32)
                       + jnp.dot(values[CMP_STRIDE:].reshape(count, half_values), comp_value_weight[half_values:], preferred_element_type=jnp.float32)).astype(jnp.bfloat16)
        group_queries = split_queries[:, group]
        blocks = group_queries.reshape(N_SEQ, Q_DEV * per_group, HEAD_QK)
        compressed_out = lax.map(lambda block: attend(block, comp_keys, comp_values, True), blocks)
        key_blocks = keys.reshape(CACHE // SEL_BLOCK, SEL_BLOCK, HEAD_QK)
        value_block_list = values.reshape(CACHE // SEL_BLOCK, SEL_BLOCK, HEAD_V)
        tiles = group_queries.reshape(QUERIES // TILE, TILE * per_group, HEAD_QK)

        def pick(inputs):
            tile, chosen = inputs
            chosen_keys = key_blocks[chosen].reshape(TOPN * SEL_BLOCK, HEAD_QK)
            chosen_values = value_block_list[chosen].reshape(TOPN * SEL_BLOCK, HEAD_V)
            return attend(tile, chosen_keys, chosen_values, True)

        selected_out = lax.map(pick, (tiles, select_blocks[:, group]))
        joined_keys = jnp.concatenate([keys[CACHE - WINDOW:], fresh_keys])
        joined_values = jnp.concatenate([values[CACHE - WINDOW:], fresh_values])

        def slide(inputs):
            index, block = inputs
            start = (index * Q_DEV).astype(jnp.int32)
            window_keys = lax.dynamic_slice_in_dim(joined_keys, start, span, 0)
            window_values = lax.dynamic_slice_in_dim(joined_values, start, span, 0)
            return attend(block, window_keys, window_values, near_rows)

        window_out = lax.map(slide, (jnp.arange(N_SEQ, dtype=jnp.int32), blocks))
        results.append((compressed_out.reshape(QUERIES, per_group, HEAD_V),
                        selected_out.reshape(QUERIES, per_group, HEAD_V),
                        window_out.reshape(QUERIES, per_group, HEAD_V)))
    compressed_all = jnp.concatenate([item[0] for item in results], axis=1)
    selected_all = jnp.concatenate([item[1] for item in results], axis=1)
    window_all = jnp.concatenate([item[2] for item in results], axis=1)
    logits = jnp.einsum("thd,hdb->thb", queries.reshape(QUERIES, HEADS, HEAD_QK).astype(jnp.float32), gate_weight.astype(jnp.float32))
    gates = jax.nn.sigmoid(logits)
    mixed = gates[:, :, 0:1] * compressed_all + gates[:, :, 1:2] * selected_all + gates[:, :, 2:3] * window_all
    return mixed.astype(jnp.bfloat16).reshape(QUERIES, HEADS * HEAD_V)
```

```python
import functools

import jax
import jax.numpy as jnp
from jax import lax
from jax.experimental import pallas as pl
from jax.experimental.pallas import tpu as pltpu
from jax.sharding import PartitionSpec as P

CMP_STRIDE = 16
SEL_BLOCK = 64
WINDOW = 512


MASKED = -1e30


def passed_along(block, axis, distance):
    devices = range(lax.axis_size(axis))
    route = [((i - distance) % len(devices), i) for i in devices]
    return lax.ppermute(block, axis, route)


def from_behind(x, axis, by):
    peers = lax.axis_size(axis)
    pairs = [(i, i + by) for i in range(peers) if 0 <= i + by < peers]
    return lax.ppermute(x, axis, pairs)


def pack_rows(keys, values):
    return jnp.concatenate([keys.reshape(-1), values.reshape(-1)])


def unpack_rows(flat, count, key_width, value_width):
    keys = flat[: count * key_width].reshape(count, key_width)
    values = flat[count * key_width : count * (key_width + value_width)].reshape(count, value_width)
    return (keys, values)


def finish_rows(scores, values):
    top = jnp.max(scores, axis=-1, keepdims=True)
    weights = jnp.exp(scores - top)
    total = jnp.sum(weights, axis=-1, keepdims=True)
    mixed = jnp.matmul(weights.astype(jnp.bfloat16), values, preferred_element_type=jnp.float32)
    return mixed / total


def shards_by_request(
    queries,
    cache_keys,
    cache_values,
    incoming_keys,
    new_values,
    comp_key_weight,
    comp_value_weight,
    select_blocks,
    gate_weight,
):
    heads, key_width, _ = gate_weight.shape
    value_width = cache_values.shape[1]
    query_count = queries.shape[0]
    cache_count = cache_keys.shape[0]
    ranks = lax.axis_size("seq")
    place = lax.axis_index("seq")
    scale = key_width ** (-0.5)
    rows = queries.reshape(query_count * heads, key_width)
    row_total = rows.shape[0]
    stretch_pos = place * query_count + jnp.arange(query_count, dtype=jnp.int32)
    lookback_length = -(-WINDOW // query_count)
    weight_keys, weight_values = (
        lax.all_gather(comp_key_weight, "kv", axis=0, tiled=True),
        lax.all_gather(comp_value_weight, "kv", axis=0, tiled=True),
    )
    tail_pack = pack_rows(cache_keys[cache_count - WINDOW :], cache_values[cache_count - WINDOW :])
    moved_tail = passed_along(tail_pack, "seq", 1)
    before_keys, before_values = unpack_rows(moved_tail, WINDOW, key_width, value_width)
    edge_keys = before_keys[WINDOW - CMP_STRIDE :]
    edge_values = before_values[WINDOW - CMP_STRIDE :]
    held_tail = jnp.where(place == 0, moved_tail, jnp.zeros_like(moved_tail))
    tail_size = held_tail.shape[0]
    tail_flat = held_tail
    near_keys = []
    near_values = []
    nearby_positions = []
    near_valid = []
    own = pack_rows(incoming_keys, new_values)
    own_size = own.shape[0]
    for back in range(lookback_length, 0, -1):
        moved = from_behind(jnp.concatenate([own, held_tail]), "seq", back)
        got_keys, got_values = unpack_rows(moved, query_count, key_width, value_width)
        tail_flat = jnp.where(place == back, moved[own_size : own_size + tail_size], tail_flat)
        near_keys.append(got_keys)
        near_values.append(got_values)
        nearby_positions.append(
            (place - back) * query_count + jnp.arange(query_count, dtype=jnp.int32)
        )
        near_valid.append(jnp.broadcast_to(place >= back, (query_count,)))
    tail_keys, tail_values = unpack_rows(tail_flat, WINDOW, key_width, value_width)
    near_keys.append(tail_keys)
    near_values.append(tail_values)
    nearby_positions.append(jnp.arange(WINDOW, dtype=jnp.int32) - WINDOW)
    near_valid.append(jnp.ones((WINDOW,), dtype=bool))
    near_keys.append(incoming_keys)
    near_values.append(new_values)
    nearby_positions.append(stretch_pos)
    near_valid.append(jnp.ones((query_count,), dtype=bool))
    half_keys = CMP_STRIDE * key_width
    half_values = CMP_STRIDE * value_width
    lead_keys = jnp.concatenate([edge_keys, cache_keys[: cache_count - CMP_STRIDE]]).reshape(
        -1, half_keys
    )
    lead_values = jnp.concatenate([edge_values, cache_values[: cache_count - CMP_STRIDE]]).reshape(
        -1, half_values
    )
    comp_keys = (
        jnp.dot(lead_keys, weight_keys[:half_keys], preferred_element_type=jnp.float32)
        + jnp.dot(
            cache_keys.reshape(-1, half_keys),
            weight_keys[half_keys:],
            preferred_element_type=jnp.float32,
        )
    ).astype(jnp.bfloat16)
    comp_values = (
        jnp.dot(lead_values, weight_values[:half_values], preferred_element_type=jnp.float32)
        + jnp.dot(
            cache_values.reshape(-1, half_values),
            weight_values[half_values:],
            preferred_element_type=jnp.float32,
        )
    ).astype(jnp.bfloat16)
    start = jnp.int32(0)
    top = jnp.full((row_total,), MASKED, jnp.float32)
    total = jnp.zeros((row_total,), jnp.float32)
    summed = jnp.zeros((row_total, value_width), jnp.float32)
    keys = lax.all_gather(comp_keys, "seq", axis=0, tiled=True)
    values = lax.all_gather(comp_values, "seq", axis=0, tiled=True)
    length = keys.shape[0]
    block = length
    for size in (1024, 512, 256, 128):
        if length % size == 0:
            block = size
            break
    for index in range(length // block):
        key_block = keys[index * block : (index + 1) * block]
        value_block = values[index * block : (index + 1) * block]
        scores = (
            jnp.einsum("rd,kd->rk", rows, key_block, preferred_element_type=jnp.float32) * scale
        )
        key_at = start + index * block + jnp.arange(block, dtype=jnp.int32)
        scores = jnp.where(key_at[None, :] > 0, scores, MASKED)
        newtop = jnp.maximum(top, jnp.max(scores, axis=1))
        factor = jnp.exp(top - newtop)
        weights = jnp.exp(scores - newtop[:, None])
        total = total * factor + jnp.sum(weights, axis=1)
        summed = summed * factor[:, None] + jnp.dot(
            weights.astype(jnp.bfloat16), value_block, preferred_element_type=jnp.float32
        )
        top = newtop
    top, total, summed = (top, total, summed)
    compressed_out = summed / total[:, None]
    chosen = select_blocks.reshape(-1)
    shard_blocks = cache_count // SEL_BLOCK
    capacity = max(2, 2 * chosen.shape[0] // ranks)
    owner = chosen // shard_blocks
    local = chosen - owner * shard_blocks
    onehot = (owner[:, None] == jnp.arange(ranks, dtype=jnp.int32)[None, :]).astype(jnp.int32)
    position = jnp.sum((jnp.cumsum(onehot, axis=0) - 1) * onehot, axis=1)
    request = jnp.full((ranks, capacity), -1, jnp.int32).at[owner, position].set(local)
    key_blocks = cache_keys.reshape(shard_blocks, SEL_BLOCK, key_width)
    value_block_list = cache_values.reshape(shard_blocks, SEL_BLOCK, value_width)
    safe = jnp.clip(
        lax.all_to_all(request, "seq", split_axis=0, concat_axis=0, tiled=True), 0, shard_blocks - 1
    )
    got_keys = lax.all_to_all(key_blocks[safe], "seq", split_axis=0, concat_axis=0, tiled=True)
    got_values = lax.all_to_all(
        value_block_list[safe], "seq", split_axis=0, concat_axis=0, tiled=True
    )
    where_at = owner * capacity + position
    tile_count = select_blocks.shape[0]
    gathered_keys = got_keys.reshape(ranks * capacity, SEL_BLOCK, key_width)[where_at]
    picked_values = got_values.reshape(ranks * capacity, SEL_BLOCK, value_width)[where_at]
    gathered_keys, picked_values = (
        gathered_keys.reshape(tile_count, -1, key_width),
        picked_values.reshape(tile_count, -1, value_width),
    )
    tile_count = gathered_keys.shape[0]
    tile_row_count = rows.reshape(tile_count, -1, key_width)
    tile_scores = (
        jnp.einsum(
            "izu,ixu->izx", tile_row_count, gathered_keys, preferred_element_type=jnp.float32
        )
        * scale
    )
    selected_out = finish_rows(tile_scores, picked_values).reshape(row_total, value_width)
    context_keys = jnp.concatenate(near_keys)
    context_values = jnp.concatenate(near_values)
    context_positions = jnp.concatenate(nearby_positions)
    context_valid = jnp.concatenate(near_valid)
    sliding_scores = (
        jnp.einsum("rd,kd->rk", rows, context_keys, preferred_element_type=jnp.float32) * scale
    )
    allowed = (
        context_valid[None, :]
        & (context_positions[None, :] <= stretch_pos[:, None])
        & (context_positions[None, :] > stretch_pos[:, None] - WINDOW)
    )
    sliding_scores = jnp.where(
        allowed[:, None, :], sliding_scores.reshape(query_count, heads, -1), MASKED
    )
    window_out = finish_rows(sliding_scores.reshape(row_total, -1), context_values)
    logits = jnp.einsum(
        "thd,hdb->thb",
        queries.reshape(query_count, heads, key_width),
        gate_weight,
        preferred_element_type=jnp.float32,
    )
    gates = jax.nn.sigmoid(logits)
    mixed = (
        gates[:, :, 0:1] * compressed_out.reshape(query_count, heads, value_width)
        + gates[:, :, 1:2] * selected_out.reshape(query_count, heads, value_width)
        + gates[:, :, 2:3] * window_out.reshape(query_count, heads, value_width)
    )
    return mixed.astype(jnp.bfloat16).reshape(query_count, heads * value_width)


CORES = 2
LOG2E = 1.4426950408889634
MESH = pl.DeviceIdType.MESH


def gather_kernel(
    n_seq,
    n_kv,
    hops,
    ck,
    cv,
    klo,
    ik,
    iv,
    iklo,
    wk,
    wv,
    ckr,
    cvr,
    kh_out,
    v_out,
    kl_out,
    nkh_out,
    nv_out,
    nkl_out,
    compk_out,
    compv_out,
    ck_vm,
    cv_vm,
    klo_vm,
    ik_vm,
    iv_vm,
    iklo_vm,
    lhs_k,
    lhs_v,
    wk_all,
    wv_all,
    compk_vm,
    compv_vm,
    local_sem,
    own_sem,
    kv_send,
    kv_recv,
    new_send,
    new_recv,
    edge_send,
    edge_recv,
    w_send,
    w_recv,
    comp_send,
    comp_recv,
):
    me = lax.axis_index("seq")
    group = lax.axis_index("kv")
    z = me // CORES
    core = lax.rem(me, CORES)
    chips = n_seq // CORES
    mate = z * CORES + 1 - core
    left = lax.rem(me - CORES + n_seq, n_seq)
    right = lax.rem(me + CORES, n_seq)
    width_v = cv.shape[1]
    rows = ckr.shape[0]

    barrier = pltpu.get_barrier_semaphore()
    for d in range(1, n_seq):
        pl.semaphore_signal(
            barrier, inc=1, device_id={"seq": lax.rem(me + d, n_seq)}, device_id_type=MESH
        )
    for d in range(1, n_kv):
        pl.semaphore_signal(
            barrier, inc=1, device_id={"kv": lax.rem(group + d, n_kv)}, device_id_type=MESH
        )

    loads = [
        (ck, ck_vm),
        (cv, cv_vm),
        (klo, klo_vm),
        (ik, ik_vm),
        (iv, iv_vm),
        (iklo, iklo_vm),
        (ckr, lhs_k.at[pl.ds(16, rows)]),
        (cvr, lhs_v.at[pl.ds(16, rows)]),
    ]
    half_k = wk.shape[0] // CORES
    half_v = wv.shape[0] // CORES
    for half in range(CORES):
        loads.append((wk.at[pl.ds(half * half_k, half_k)], wk_all.at[group, half]))
        loads.append((wv.at[pl.ds(half * half_v, half_v)], wv_all.at[group, half]))
    load_copies = [pltpu.make_async_copy(a, b, local_sem.at[n]) for n, (a, b) in enumerate(loads)]
    for copy in load_copies:
        copy.start()

    pl.semaphore_wait(barrier, n_seq - 1 + n_kv - 1)

    old_outs = (kh_out, v_out, kl_out)
    new_outs = (nkh_out, nv_out, nkl_out)
    old_own = (ck.at[:, pl.ds(0, width_v)], cv, klo)
    new_own = (ik.at[:, pl.ds(0, width_v)], iv, iklo)
    route = (left, right, mate)

    def message(outs, own, sends, recvs, slot, way, part):
        source = outs[part].at[slot] if own is None else own[part]
        return pltpu.make_async_remote_copy(
            src_ref=source,
            dst_ref=outs[part].at[slot],
            send_sem=sends.at[way, slot, part],
            recv_sem=recvs.at[slot, part],
            device_id={"seq": route[way]},
            device_id_type=MESH,
        )

    def old_msg(slot, way, part, own=None):
        return message(old_outs, own, kv_send, kv_recv, slot, way, part)

    def new_msg(slot, way, part, own=None):
        return message(new_outs, own, new_send, new_recv, slot, way, part)

    PARTS = range(3)

    def start(make, slot, way, own=None):
        for part in PARTS:
            make(slot, way, part, own).start()

    def recv(make, slot):
        for part in PARTS:
            make(slot, 2, part).wait_recv()

    def sent(make, slot, way, own=None):
        for part in PARTS:
            make(slot, way, part, own).wait_send()

    @pl.when(z < chips - 1)
    def _():
        start(new_msg, me, 1, new_own)

    start(new_msg, me, 2, new_own)

    nxt = lax.rem(me + 1, n_seq)
    prev = lax.rem(me + n_seq - 1, n_seq)
    edges = [
        pltpu.make_async_remote_copy(
            src_ref=src.at[pl.ds(rows - 16, 16)],
            dst_ref=dst.at[pl.ds(0, 16)],
            send_sem=edge_send.at[n],
            recv_sem=edge_recv.at[n],
            device_id={"seq": nxt},
            device_id_type=MESH,
        )
        for n, (src, dst) in enumerate(((ckr, lhs_k), (cvr, lhs_v)))
    ]
    for copy in edges:
        copy.start()

    @pl.when(z < chips - 1)
    def _():
        start(old_msg, me, 1, old_own)

    @pl.when(z > 0)
    def _():
        start(old_msg, me, 0, old_own)

    w_all = (wk_all, wv_all)
    w_own = (
        wk.at[pl.ds(pl.multiple_of(core * half_k, half_k), half_k)],
        wv.at[pl.ds(pl.multiple_of(core * half_v, half_v), half_v)],
    )

    def w_msg(d, part):
        return pltpu.make_async_remote_copy(
            src_ref=w_own[part],
            dst_ref=w_all[part].at[group, core],
            send_sem=w_send.at[d - 1, part],
            recv_sem=w_recv.at[group, core, part],
            device_id={"kv": lax.rem(group + d, n_kv)},
            device_id_type=MESH,
        )

    def w_arrived(who, half, part):
        return pltpu.make_async_remote_copy(
            src_ref=w_all[part].at[who, half],
            dst_ref=w_all[part].at[who, half],
            send_sem=w_send.at[n_kv - 1 + lax.rem(who - group + n_kv, n_kv) - 1, part],
            recv_sem=w_recv.at[who, half, part],
            device_id={"seq": mate},
            device_id_type=MESH,
        )

    for d in range(1, n_kv):
        for part in range(2):
            w_msg(d, part).start()

    start(old_msg, me, 2, old_own)

    for copy in load_copies:
        copy.wait()
    keeps = [
        (ck_vm.at[:, pl.ds(0, width_v)], kh_out.at[me]),
        (cv_vm, v_out.at[me]),
        (klo_vm, kl_out.at[me]),
        (ik_vm.at[:, pl.ds(0, width_v)], nkh_out.at[me]),
        (iv_vm, nv_out.at[me]),
        (iklo_vm, nkl_out.at[me]),
    ]
    keep_copies = [pltpu.make_async_copy(a, b, own_sem.at[n]) for n, (a, b) in enumerate(keeps)]
    for copy in keep_copies:
        copy.start()

    for d in range(1, min(hops, chips - 1) + 1):

        @pl.when(z >= d)
        def _():
            slot = me - CORES * d
            recv(new_msg, slot)
            if d < hops:

                @pl.when(z < chips - 1)
                def _():
                    start(new_msg, slot, 1)

            start(new_msg, slot, 2)

    def relay(d):
        @pl.when(z >= d)
        def _():
            slot = me - CORES * d
            recv(old_msg, slot)

            @pl.when(z < chips - 1)
            def _():
                start(old_msg, slot, 1)

            start(old_msg, slot, 2)

        @pl.when(z + d < chips)
        def _():
            slot = me + CORES * d
            recv(old_msg, slot)

            @pl.when(z > 0)
            def _():
                start(old_msg, slot, 0)

            start(old_msg, slot, 2)

    comps = ((compk_vm, compk_out), (compv_vm, compv_out))

    def comp_msg(d, part):
        return pltpu.make_async_remote_copy(
            src_ref=comps[part][0],
            dst_ref=comps[part][1].at[me],
            send_sem=comp_send.at[d - 1, part],
            recv_sem=comp_recv.at[me, part],
            device_id={"seq": lax.rem(me + d, n_seq)},
            device_id_type=MESH,
        )

    def compress():
        for d in range(1, n_kv):
            who = lax.rem(group + n_kv - d, n_kv)
            for part in range(2):
                w_arrived(who, core, part).wait_recv()
                w_arrived(who, core, part).start()
        for d in range(1, n_kv):
            who = lax.rem(group + n_kv - d, n_kv)
            for part in range(2):
                w_arrived(who, 1 - core, part).wait_recv()
        for copy in edges:
            copy.wait_recv()
        for lhs, w, (held, _) in ((lhs_k, wk_all, comps[0]), (lhs_v, wv_all, comps[1])):
            depth = w.shape[2]
            chunks = n_kv * CORES
            sums = []
            for side in range(2):
                total = None
                for n in range(chunks // 2):
                    at = side * (chunks // 2) + n
                    term = jnp.dot(
                        lhs[:, n * depth : (n + 1) * depth],
                        w[at // CORES, at % CORES],
                        preferred_element_type=jnp.float32,
                    )
                    total = term if total is None else total + term
                sums.append(total)
            held[...] = (sums[0][15 : 15 + rows] + sums[1][16 : 16 + rows]).astype(jnp.bfloat16)
        for d in range(1, n_seq):
            for part in range(2):
                comp_msg(d, part).start()
        for part in range(2):
            pltpu.make_async_copy(comps[part][0], comps[part][1].at[me], own_sem.at[6 + part]).start()

    relay(1)
    compress()
    for d in range(2, chips):
        relay(d)

    for copy in keep_copies:
        copy.wait()
    for part in range(2):
        pltpu.make_async_copy(comps[part][0], comps[part][1].at[me], own_sem.at[6 + part]).wait()
    for zz in range(chips):
        recv(old_msg, zz * CORES + 1 - core)
    for d in range(0, min(hops, chips - 1) + 1):

        @pl.when(z >= d)
        def _():
            recv(new_msg, (z - d) * CORES + 1 - core)

    for d in range(1, n_seq):
        who = lax.rem(me + d, n_seq)
        for part in range(2):
            pltpu.make_async_remote_copy(
                src_ref=comps[part][0],
                dst_ref=comps[part][1].at[who],
                send_sem=comp_send.at[d - 1, part],
                recv_sem=comp_recv.at[who, part],
                device_id={"seq": who},
                device_id_type=MESH,
            ).wait_recv()
    for copy in edges:
        copy.wait_send()
    for d in range(1, n_kv):
        for part in range(2):
            w_msg(d, part).wait_send()
            w_arrived(lax.rem(group + n_kv - d, n_kv), core, part).wait_send()
    for d in range(1, n_seq):
        for part in range(2):
            comp_msg(d, part).wait_send()

    @pl.when(z < chips - 1)
    def _():
        sent(new_msg, me, 1, new_own)
        sent(old_msg, me, 1, old_own)

    @pl.when(z > 0)
    def _():
        sent(old_msg, me, 0, old_own)

    sent(new_msg, me, 2, new_own)
    sent(old_msg, me, 2, old_own)
    for d in range(1, chips):

        @pl.when(z >= d)
        def _():
            slot = me - CORES * d
            if d <= hops:
                sent(new_msg, slot, 2)

                if d < hops:

                    @pl.when(z < chips - 1)
                    def _():
                        sent(new_msg, slot, 1)

            sent(old_msg, slot, 2)

            @pl.when(z < chips - 1)
            def _():
                sent(old_msg, slot, 1)

        @pl.when(z + d < chips)
        def _():
            slot = me + CORES * d
            sent(old_msg, slot, 2)

            @pl.when(z > 0)
            def _():
                sent(old_msg, slot, 0)


def attend_kernel(
    heads,
    tile,
    lookback,
    sel,
    q,
    kh,
    v,
    kl,
    nkh,
    nv,
    nkl,
    compk,
    compv,
    gw,
    out,
    rows_vm,
    win_k,
    win_v,
    sel_k,
    sel_v,
):
    me = lax.axis_index("seq")
    step = pl.program_id(0)
    width = gw.shape[0]
    vw = v.shape[2]
    low = width - vw
    factor = width**-0.5 * LOG2E
    per = nkh.shape[1]
    blocks_per = per // SEL_BLOCK

    def put(dk, dv, at, khv, vv, klv):
        half = SEL_BLOCK // 2
        dk[pl.ds(at, SEL_BLOCK), 0:vw] = khv
        dk[pl.ds(at, half), vw:width] = klv[:, 0:low]
        dk[pl.ds(at + half, half), vw:width] = klv[:, low : 2 * low]
        dv[pl.ds(at, SEL_BLOCK), :] = vv

    @pl.when(step == 0)
    def _():
        total = kh.shape[0]
        for i in range(lookback + 1):
            chunk = me + i
            for b in range(blocks_per):
                at = i * per + b * SEL_BLOCK

                @pl.when(chunk < lookback)
                def _():
                    block = total - lookback * blocks_per + chunk * blocks_per + b
                    put(win_k, win_v, at, kh[block], v[block], kl[block])

                @pl.when(chunk >= lookback)
                def _():
                    slot = chunk - lookback
                    put(
                        win_k,
                        win_v,
                        at,
                        nkh[slot, b * SEL_BLOCK : (b + 1) * SEL_BLOCK],
                        nv[slot, b * SEL_BLOCK : (b + 1) * SEL_BLOCK],
                        nkl[slot, b * SEL_BLOCK // 2 : (b + 1) * SEL_BLOCK // 2],
                    )

    for h in range(heads):
        rows_vm[h * tile : (h + 1) * tile, :] = q[:, h * width : (h + 1) * width]
    picks = sel.shape[1]
    for n in range(picks):
        block = sel[step, n]
        put(sel_k, sel_v, n * SEL_BLOCK, kh[block], v[block], kl[block])

    logits = jnp.dot(rows_vm[...], gw[...], preferred_element_type=jnp.float32)
    gates = jax.nn.sigmoid(logits)
    span = WINDOW + tile
    off = pl.multiple_of(step * tile, tile)

    def attend(rows, keys, values, allowed):
        s = lax.dot_general(
            rows, keys, (((1,), (1,)), ((), ())), preferred_element_type=jnp.float32
        )
        if allowed is not None:
            s = jnp.where(allowed, s, MASKED)
        top = jnp.max(s, axis=-1, keepdims=True)
        w = jnp.exp2((s - top) * factor)
        total = jnp.sum(w, axis=-1, keepdims=True)
        o = jnp.dot(w.astype(jnp.bfloat16), values, preferred_element_type=jnp.float32)
        return o / total

    group_heads = 4
    count = group_heads * tile
    comp_n = compk.shape[0]
    comp_ok = lax.broadcasted_iota(jnp.int32, (count, comp_n), 1) > 0
    diff = lax.broadcasted_iota(jnp.int32, (count, span), 1) - lax.rem(
        lax.broadcasted_iota(jnp.int32, (count, span), 0), tile
    )
    win_ok = (diff > 0) & (diff <= WINDOW)
    for g in range(heads // group_heads):
        rows = rows_vm[g * count : (g + 1) * count, :]
        c = attend(rows, compk[...], compv[...], comp_ok)
        s = attend(rows, sel_k[...], sel_v[...], None)
        w = attend(rows, win_k[pl.ds(off, span), :], win_v[pl.ds(off, span), :], win_ok)
        for i in range(group_heads):
            h = g * group_heads + i
            a = slice(i * tile, (i + 1) * tile)
            b = slice(h * tile, (h + 1) * tile)
            mixed = (
                gates[b, 3 * h : 3 * h + 1] * c[a]
                + gates[b, 3 * h + 1 : 3 * h + 2] * s[a]
                + gates[b, 3 * h + 2 : 3 * h + 3] * w[a]
            )
            out[:, h * vw : (h + 1) * vw] = mixed.astype(out.dtype)


def pack_low(keys, vw):
    low = keys.shape[1] - vw
    part = keys[:, vw:].reshape(-1, 2, SEL_BLOCK // 2, low)
    return jnp.concatenate([part[:, 0], part[:, 1]], axis=-1).reshape(-1, 2 * low)


def shards_gathered(q, ck, cv, ik, iv, wk, wv, sel, gw):
    n_seq, n_kv = lax.axis_size("seq"), lax.axis_size("kv")
    heads, width, branches = gw.shape
    vw = cv.shape[1]
    cache, fresh = ck.shape[0], ik.shape[0]
    tiles = sel.shape[0]
    tile = fresh // tiles
    lookback = WINDOW // fresh
    hops = -(-lookback // CORES)
    rows = cache // CMP_STRIDE
    bf = jnp.bfloat16
    any_spec = pl.BlockSpec(memory_space=pl.ANY)
    half_k, half_v = wk.shape[0] // CORES, wv.shape[0] // CORES
    gathered = pl.pallas_call(
        functools.partial(gather_kernel, n_seq, n_kv, hops),
        out_shape=[
            jax.ShapeDtypeStruct((n_seq, cache, vw), bf),
            jax.ShapeDtypeStruct((n_seq, cache, vw), bf),
            jax.ShapeDtypeStruct((n_seq, cache // 2, vw), bf),
            jax.ShapeDtypeStruct((n_seq, fresh, vw), bf),
            jax.ShapeDtypeStruct((n_seq, fresh, vw), bf),
            jax.ShapeDtypeStruct((n_seq, fresh // 2, vw), bf),
            jax.ShapeDtypeStruct((n_seq, rows, width), bf),
            jax.ShapeDtypeStruct((n_seq, rows, vw), bf),
        ],
        in_specs=[any_spec] * 10,
        out_specs=[any_spec] * 8,
        scratch_shapes=[
            pltpu.VMEM((cache, width), bf),
            pltpu.VMEM((cache, vw), bf),
            pltpu.VMEM((cache // 2, vw), bf),
            pltpu.VMEM((fresh, width), bf),
            pltpu.VMEM((fresh, vw), bf),
            pltpu.VMEM((fresh // 2, vw), bf),
            pltpu.VMEM((rows + 16, CMP_STRIDE * width), bf),
            pltpu.VMEM((rows + 16, CMP_STRIDE * vw), bf),
            pltpu.VMEM((n_kv, CORES, half_k, width), bf),
            pltpu.VMEM((n_kv, CORES, half_v, vw), bf),
            pltpu.VMEM((rows, width), bf),
            pltpu.VMEM((rows, vw), bf),
            pltpu.SemaphoreType.DMA((12,)),
            pltpu.SemaphoreType.DMA((8,)),
            pltpu.SemaphoreType.DMA((3, n_seq, 3)),
            pltpu.SemaphoreType.DMA((n_seq, 3)),
            pltpu.SemaphoreType.DMA((3, n_seq, 3)),
            pltpu.SemaphoreType.DMA((n_seq, 3)),
            pltpu.SemaphoreType.DMA((2,)),
            pltpu.SemaphoreType.DMA((2,)),
            pltpu.SemaphoreType.DMA((2 * (n_kv - 1), 2)),
            pltpu.SemaphoreType.DMA((n_kv, CORES, 2)),
            pltpu.SemaphoreType.DMA((n_seq - 1, 2)),
            pltpu.SemaphoreType.DMA((n_seq, 2)),
        ],
        compiler_params=pltpu.CompilerParams(collective_id=0, has_side_effects=True),
    )(
        ck,
        cv,
        pack_low(ck, vw),
        ik,
        iv,
        pack_low(ik, vw),
        wk,
        wv,
        ck.reshape(rows, CMP_STRIDE * width),
        cv.reshape(rows, CMP_STRIDE * vw),
    )
    kh, v, kl, nkh, nv, nkl, compk, compv = gathered
    blocks = n_seq * cache // SEL_BLOCK
    kh = kh.reshape(blocks, SEL_BLOCK, vw)
    v = v.reshape(blocks, SEL_BLOCK, vw)
    kl = kl.reshape(blocks, SEL_BLOCK // 2, vw)
    compk = compk.reshape(n_seq * rows, width)
    compv = compv.reshape(n_seq * rows, vw)
    gates = jnp.transpose(gw, (1, 0, 2)).reshape(width, heads * branches)

    def whole(x):
        return pl.BlockSpec(
            x.shape, lambda i, s: (0,) * x.ndim, pipeline_mode=pl.Buffered(1)
        )

    fixed = [kh, v, kl, nkh, nv, nkl, compk, compv, gates]
    picks = sel.shape[-1]
    return pl.pallas_call(
        functools.partial(attend_kernel, heads, tile, lookback),
        out_shape=jax.ShapeDtypeStruct((fresh, heads * vw), bf),
        grid_spec=pltpu.PrefetchScalarGridSpec(
            num_scalar_prefetch=1,
            grid=(tiles,),
            in_specs=[pl.BlockSpec((tile, heads * width), lambda i, s: (i, 0))]
            + [whole(x) for x in fixed],
            out_specs=pl.BlockSpec((tile, heads * vw), lambda i, s: (i, 0)),
            scratch_shapes=[
                pltpu.VMEM((heads * tile, width), bf),
                pltpu.VMEM((fresh + WINDOW, width), bf),
                pltpu.VMEM((fresh + WINDOW, vw), bf),
                pltpu.VMEM((picks * SEL_BLOCK, width), bf),
                pltpu.VMEM((picks * SEL_BLOCK, vw), bf),
            ],
        ),
        compiler_params=pltpu.CompilerParams(vmem_limit_bytes=60 << 20),
    )(sel.reshape(tiles, picks), q, *fixed)


GATHER_BYTES = 1 << 24


def shards(queries, cache_keys, cache_values, *rest):
    ranks = lax.axis_size("seq")
    size = ranks * 2 * (cache_keys.size + cache_values.size)
    form = shards_gathered if size <= GATHER_BYTES else shards_by_request
    return form(queries, cache_keys, cache_values, *rest)


def solution(mesh):
    placed = (
        P("seq", "kv"),
        P("seq", "kv"),
        P("seq", "kv"),
        P("seq", "kv"),
        P("seq", "kv"),
        P("kv", None),
        P("kv", None),
        P("seq", "kv", None),
        P("kv", None, None),
    )
    return jax.shard_map(
        shards, mesh=mesh, in_specs=placed, out_specs=P("seq", "kv"), check_vma=False
    )
```

```python
import functools

import jax
import jax.numpy as jnp
from jax import lax
from jax.experimental import pallas as pl
from jax.experimental.pallas import tpu as pltpu
from jax.sharding import PartitionSpec as P

CMP_STRIDE = 16
SEL_BLOCK = 64
WINDOW = 512


MASKED = -1e30


def passed_along(block, axis, distance):
    devices = range(lax.axis_size(axis))
    route = [((i - distance) % len(devices), i) for i in devices]
    return lax.ppermute(block, axis, route)


def from_behind(x, axis, by):
    peers = lax.axis_size(axis)
    pairs = [(i, i + by) for i in range(peers) if 0 <= i + by < peers]
    return lax.ppermute(x, axis, pairs)


def pack_rows(keys, values):
    return jnp.concatenate([keys.reshape(-1), values.reshape(-1)])


def unpack_rows(flat, count, key_width, value_width):
    keys = flat[: count * key_width].reshape(count, key_width)
    values = flat[count * key_width : count * (key_width + value_width)].reshape(count, value_width)
    return (keys, values)


def finish_rows(scores, values):
    top = jnp.max(scores, axis=-1, keepdims=True)
    weights = jnp.exp(scores - top)
    total = jnp.sum(weights, axis=-1, keepdims=True)
    mixed = jnp.matmul(weights.astype(jnp.bfloat16), values, preferred_element_type=jnp.float32)
    return mixed / total


def shards_by_request(
    queries,
    cache_keys,
    cache_values,
    incoming_keys,
    new_values,
    comp_key_weight,
    comp_value_weight,
    select_blocks,
    gate_weight,
):
    heads, key_width, _ = gate_weight.shape
    value_width = cache_values.shape[1]
    query_count = queries.shape[0]
    cache_count = cache_keys.shape[0]
    ranks = lax.axis_size("seq")
    place = lax.axis_index("seq")
    scale = key_width ** (-0.5)
    rows = queries.reshape(query_count * heads, key_width)
    row_total = rows.shape[0]
    stretch_pos = place * query_count + jnp.arange(query_count, dtype=jnp.int32)
    lookback_length = -(-WINDOW // query_count)
    weight_keys, weight_values = (
        lax.all_gather(comp_key_weight, "kv", axis=0, tiled=True),
        lax.all_gather(comp_value_weight, "kv", axis=0, tiled=True),
    )
    tail_pack = pack_rows(cache_keys[cache_count - WINDOW :], cache_values[cache_count - WINDOW :])
    moved_tail = passed_along(tail_pack, "seq", 1)
    before_keys, before_values = unpack_rows(moved_tail, WINDOW, key_width, value_width)
    edge_keys = before_keys[WINDOW - CMP_STRIDE :]
    edge_values = before_values[WINDOW - CMP_STRIDE :]
    held_tail = jnp.where(place == 0, moved_tail, jnp.zeros_like(moved_tail))
    tail_size = held_tail.shape[0]
    tail_flat = held_tail
    near_keys = []
    near_values = []
    nearby_positions = []
    near_valid = []
    own = pack_rows(incoming_keys, new_values)
    own_size = own.shape[0]
    for back in range(lookback_length, 0, -1):
        moved = from_behind(jnp.concatenate([own, held_tail]), "seq", back)
        got_keys, got_values = unpack_rows(moved, query_count, key_width, value_width)
        tail_flat = jnp.where(place == back, moved[own_size : own_size + tail_size], tail_flat)
        near_keys.append(got_keys)
        near_values.append(got_values)
        nearby_positions.append(
            (place - back) * query_count + jnp.arange(query_count, dtype=jnp.int32)
        )
        near_valid.append(jnp.broadcast_to(place >= back, (query_count,)))
    tail_keys, tail_values = unpack_rows(tail_flat, WINDOW, key_width, value_width)
    near_keys.append(tail_keys)
    near_values.append(tail_values)
    nearby_positions.append(jnp.arange(WINDOW, dtype=jnp.int32) - WINDOW)
    near_valid.append(jnp.ones((WINDOW,), dtype=bool))
    near_keys.append(incoming_keys)
    near_values.append(new_values)
    nearby_positions.append(stretch_pos)
    near_valid.append(jnp.ones((query_count,), dtype=bool))
    half_keys = CMP_STRIDE * key_width
    half_values = CMP_STRIDE * value_width
    lead_keys = jnp.concatenate([edge_keys, cache_keys[: cache_count - CMP_STRIDE]]).reshape(
        -1, half_keys
    )
    lead_values = jnp.concatenate([edge_values, cache_values[: cache_count - CMP_STRIDE]]).reshape(
        -1, half_values
    )
    comp_keys = (
        jnp.dot(lead_keys, weight_keys[:half_keys], preferred_element_type=jnp.float32)
        + jnp.dot(
            cache_keys.reshape(-1, half_keys),
            weight_keys[half_keys:],
            preferred_element_type=jnp.float32,
        )
    ).astype(jnp.bfloat16)
    comp_values = (
        jnp.dot(lead_values, weight_values[:half_values], preferred_element_type=jnp.float32)
        + jnp.dot(
            cache_values.reshape(-1, half_values),
            weight_values[half_values:],
            preferred_element_type=jnp.float32,
        )
    ).astype(jnp.bfloat16)
    start = jnp.int32(0)
    top = jnp.full((row_total,), MASKED, jnp.float32)
    total = jnp.zeros((row_total,), jnp.float32)
    summed = jnp.zeros((row_total, value_width), jnp.float32)
    keys = lax.all_gather(comp_keys, "seq", axis=0, tiled=True)
    values = lax.all_gather(comp_values, "seq", axis=0, tiled=True)
    length = keys.shape[0]
    block = length
    for size in (1024, 512, 256, 128):
        if length % size == 0:
            block = size
            break
    for index in range(length // block):
        key_block = keys[index * block : (index + 1) * block]
        value_block = values[index * block : (index + 1) * block]
        scores = (
            jnp.einsum("rd,kd->rk", rows, key_block, preferred_element_type=jnp.float32) * scale
        )
        key_at = start + index * block + jnp.arange(block, dtype=jnp.int32)
        scores = jnp.where(key_at[None, :] > 0, scores, MASKED)
        newtop = jnp.maximum(top, jnp.max(scores, axis=1))
        factor = jnp.exp(top - newtop)
        weights = jnp.exp(scores - newtop[:, None])
        total = total * factor + jnp.sum(weights, axis=1)
        summed = summed * factor[:, None] + jnp.dot(
            weights.astype(jnp.bfloat16), value_block, preferred_element_type=jnp.float32
        )
        top = newtop
    top, total, summed = (top, total, summed)
    compressed_out = summed / total[:, None]
    chosen = select_blocks.reshape(-1)
    shard_blocks = cache_count // SEL_BLOCK
    capacity = max(2, 2 * chosen.shape[0] // ranks)
    owner = chosen // shard_blocks
    local = chosen - owner * shard_blocks
    onehot = (owner[:, None] == jnp.arange(ranks, dtype=jnp.int32)[None, :]).astype(jnp.int32)
    position = jnp.sum((jnp.cumsum(onehot, axis=0) - 1) * onehot, axis=1)
    request = jnp.full((ranks, capacity), -1, jnp.int32).at[owner, position].set(local)
    key_blocks = cache_keys.reshape(shard_blocks, SEL_BLOCK, key_width)
    value_block_list = cache_values.reshape(shard_blocks, SEL_BLOCK, value_width)
    safe = jnp.clip(
        lax.all_to_all(request, "seq", split_axis=0, concat_axis=0, tiled=True), 0, shard_blocks - 1
    )
    got_keys = lax.all_to_all(key_blocks[safe], "seq", split_axis=0, concat_axis=0, tiled=True)
    got_values = lax.all_to_all(
        value_block_list[safe], "seq", split_axis=0, concat_axis=0, tiled=True
    )
    where_at = owner * capacity + position
    tile_count = select_blocks.shape[0]
    gathered_keys = got_keys.reshape(ranks * capacity, SEL_BLOCK, key_width)[where_at]
    picked_values = got_values.reshape(ranks * capacity, SEL_BLOCK, value_width)[where_at]
    gathered_keys, picked_values = (
        gathered_keys.reshape(tile_count, -1, key_width),
        picked_values.reshape(tile_count, -1, value_width),
    )
    tile_count = gathered_keys.shape[0]
    tile_row_count = rows.reshape(tile_count, -1, key_width)
    tile_scores = (
        jnp.einsum(
            "izu,ixu->izx", tile_row_count, gathered_keys, preferred_element_type=jnp.float32
        )
        * scale
    )
    selected_out = finish_rows(tile_scores, picked_values).reshape(row_total, value_width)
    context_keys = jnp.concatenate(near_keys)
    context_values = jnp.concatenate(near_values)
    context_positions = jnp.concatenate(nearby_positions)
    context_valid = jnp.concatenate(near_valid)
    sliding_scores = (
        jnp.einsum("rd,kd->rk", rows, context_keys, preferred_element_type=jnp.float32) * scale
    )
    allowed = (
        context_valid[None, :]
        & (context_positions[None, :] <= stretch_pos[:, None])
        & (context_positions[None, :] > stretch_pos[:, None] - WINDOW)
    )
    sliding_scores = jnp.where(
        allowed[:, None, :], sliding_scores.reshape(query_count, heads, -1), MASKED
    )
    window_out = finish_rows(sliding_scores.reshape(row_total, -1), context_values)
    logits = jnp.einsum(
        "thd,hdb->thb",
        queries.reshape(query_count, heads, key_width),
        gate_weight,
        preferred_element_type=jnp.float32,
    )
    gates = jax.nn.sigmoid(logits)
    mixed = (
        gates[:, :, 0:1] * compressed_out.reshape(query_count, heads, value_width)
        + gates[:, :, 1:2] * selected_out.reshape(query_count, heads, value_width)
        + gates[:, :, 2:3] * window_out.reshape(query_count, heads, value_width)
    )
    return mixed.astype(jnp.bfloat16).reshape(query_count, heads * value_width)


CORES = 2
LOG2E = 1.4426950408889634
MESH = pl.DeviceIdType.MESH


def fused_kernel(
    n_seq,
    n_kv,
    tiles,
    sel,
    q,
    ckt,
    cv,
    ikt,
    iv,
    wkt,
    wv,
    gw,
    out,
    q_vm,
    ckt_vm,
    ikt_vm,
    gw_vm,
    kh,
    v,
    kl,
    nkh,
    nv,
    nkl,
    k_ext,
    v_ext,
    perm,
    lhs_k,
    lhs_v,
    wk_all,
    wv_all,
    compk_vm,
    compv_vm,
    compk,
    compv,
    rows_vm,
    gates_vm,
    acc,
    win_k,
    win_v,
    sel_k,
    sel_v,
    local_sem,
    own_sem,
    kv_send,
    kv_recv,
    new_send,
    new_recv,
    w_send,
    w_recv,
    comp_send,
    comp_recv,
):
    me = lax.axis_index("seq")
    group = lax.axis_index("kv")
    z = me // CORES
    core = lax.rem(me, CORES)
    chips = n_seq // CORES
    mate = z * CORES + 1 - core
    left = lax.rem(me - CORES + n_seq, n_seq)
    right = lax.rem(me + CORES, n_seq)
    route = (left, right, mate)
    width, cache = ckt.shape
    fresh = ikt.shape[1]
    vw = v.shape[2]
    low = width - vw
    per = cache // SEL_BLOCK
    new_per = fresh // SEL_BLOCK
    half_block = SEL_BLOCK // 2
    heads = q.shape[1] // width
    tile = fresh // tiles
    count = heads * tile
    lookback = WINDOW // fresh
    hops = -(-lookback // CORES)
    chunks = cache // CMP_STRIDE
    pad = chunks + CMP_STRIDE
    factor = width**-0.5 * LOG2E

    barrier = pltpu.get_barrier_semaphore()
    for d in range(1, n_seq):
        pl.semaphore_signal(
            barrier, inc=1, device_id={"seq": lax.rem(me + d, n_seq)}, device_id_type=MESH
        )
    for d in range(1, n_kv):
        pl.semaphore_signal(
            barrier, inc=1, device_id={"kv": lax.rem(group + d, n_kv)}, device_id_type=MESH
        )

    half_k = wkt.shape[1] // CORES
    half_v = wv.shape[0] // CORES
    loads = [
        (cv, v.at[pl.ds(me * per, per)]),
        (iv, nv.at[pl.ds(me * new_per, new_per)]),
        (ckt, ckt_vm),
        (ikt, ikt_vm),
        (q, q_vm),
        (gw, gw_vm),
    ]
    for half in range(CORES):
        loads.append((wkt.at[:, pl.ds(half * half_k, half_k)], wk_all.at[group, half]))
        loads.append((wv.at[pl.ds(half * half_v, half_v)], wv_all.at[group, half]))
    load_copies = [pltpu.make_async_copy(a, b, local_sem.at[n]) for n, (a, b) in enumerate(loads)]
    for copy in load_copies:
        copy.start()

    old = (v, kh, kl)
    new = (nv, nkh, nkl)

    def piece(half):
        return per // 2 * half, per // 2

    def old_msg(slot, way, part, half):
        at, size = piece(half)
        ref = old[part].at[pl.ds(slot * per + at, size)]
        return pltpu.make_async_remote_copy(
            src_ref=ref,
            dst_ref=ref,
            send_sem=kv_send.at[way, slot, part, half],
            recv_sem=kv_recv.at[slot, part, half],
            device_id={"seq": route[way]},
            device_id_type=MESH,
        )

    def new_msg(slot, way, part, half):
        ref = new[part].at[pl.ds(slot * new_per, new_per)]
        return pltpu.make_async_remote_copy(
            src_ref=ref,
            dst_ref=ref,
            send_sem=new_send.at[way, slot, part],
            recv_sem=new_recv.at[slot, part],
            device_id={"seq": route[way]},
            device_id_type=MESH,
        )

    def start(make, slot, way, half, parts=range(3)):
        for part in parts:
            make(slot, way, part, half).start()

    def recv(make, slot, half):
        for part in range(3):
            make(slot, 2, part, half).wait_recv()

    def sent(make, slot, way, half):
        for part in range(3):
            make(slot, way, part, half).wait_send()

    def start_own(parts):
        for half in (1, 0):

            @pl.when(z < chips - 1)
            def _():
                start(old_msg, me, 1, half, parts)

            @pl.when(z > 0)
            def _():
                start(old_msg, me, 0, half, parts)

            start(old_msg, me, 2, half, parts)

    w_all = (wk_all, wv_all)
    w_own = (
        wkt.at[:, pl.ds(pl.multiple_of(core * half_k, half_k), half_k)],
        wv.at[pl.ds(pl.multiple_of(core * half_v, half_v), half_v)],
    )

    def w_msg(d, part):
        return pltpu.make_async_remote_copy(
            src_ref=w_own[part],
            dst_ref=w_all[part].at[group, core],
            send_sem=w_send.at[d - 1, part],
            recv_sem=w_recv.at[group, core, part],
            device_id={"kv": lax.rem(group + d, n_kv)},
            device_id_type=MESH,
        )

    def w_arrived(who, half, part):
        return pltpu.make_async_remote_copy(
            src_ref=w_all[part].at[who, half],
            dst_ref=w_all[part].at[who, half],
            send_sem=w_send.at[n_kv - 1 + lax.rem(who - group + n_kv, n_kv) - 1, part],
            recv_sem=w_recv.at[who, half, part],
            device_id={"seq": mate},
            device_id_type=MESH,
        )

    load_copies[0].wait()
    load_copies[1].wait()
    pl.semaphore_wait(barrier, n_seq - 1 + n_kv - 1)
    start_own((0,))
    for d in range(1, n_kv):
        for part in range(2):
            w_msg(d, part).start()

    def pack(keys, blocks, hi, lo, at):
        hi[pl.ds(at, blocks)] = keys[:, 0:vw].reshape(blocks, SEL_BLOCK, vw)
        part = keys[:, vw:width].reshape(blocks, 2, half_block, low)
        lo[pl.ds(at, blocks)] = jnp.concatenate([part[:, 0], part[:, 1]], axis=-1)

    load_copies[2].wait()
    keys = ckt_vm[...].T
    pack(keys, per, kh, kl, me * per)
    k_ext[CMP_STRIDE:, :] = keys
    load_copies[3].wait()
    pack(ikt_vm[...].T, new_per, nkh, nkl, me * new_per)
    v_ext[CMP_STRIDE:, :] = v[pl.ds(me * per, per)].reshape(cache, vw)
    for copy in load_copies[4:]:
        copy.wait()

    @pl.when(z < chips - 1)
    def _():
        start(new_msg, me, 1, 0)

    start_own((1, 2))
    start(new_msg, me, 2, 0)

    @pl.loop(0, tiles)
    def _(t):
        part = q_vm[pl.ds(pl.multiple_of(t * tile, tile), tile), :]
        for h in range(heads):
            at = pl.multiple_of(t * count + h * tile, tile)
            rows_vm[pl.ds(at, tile), :] = part[:, h * width : (h + 1) * width]

    logits = lax.dot_general(
        rows_vm[...], gw_vm[...], (((1,), (1,)), ((), ())), preferred_element_type=jnp.float32
    )
    gates_vm[...] = jax.nn.sigmoid(logits)
    lag = lax.broadcasted_iota(jnp.int32, (pad, cache + CMP_STRIDE), 1)
    lag = lag - CMP_STRIDE * lax.broadcasted_iota(jnp.int32, lag.shape, 0)

    @pl.loop(0, CMP_STRIDE)
    def _(p):
        at = pl.multiple_of(p * pad, CMP_STRIDE)
        perm[pl.ds(at, pad), :] = jnp.where(lag == p, 1.0, 0.0).astype(jnp.bfloat16)

    for d in range(1, min(hops, chips - 1) + 1):

        @pl.when(z >= d)
        def _():
            slot = me - CORES * d
            recv(new_msg, slot, 0)
            if d < hops:

                @pl.when(z < chips - 1)
                def _():
                    start(new_msg, slot, 1, 0)

            start(new_msg, slot, 2, 0)

    def relay(d, half):
        @pl.when(z >= d)
        def _():
            slot = me - CORES * d
            recv(old_msg, slot, half)

            @pl.when(z < chips - 1)
            def _():
                start(old_msg, slot, 1, half)

            start(old_msg, slot, 2, half)

        @pl.when(z + d < chips)
        def _():
            slot = me + CORES * d
            recv(old_msg, slot, half)

            @pl.when(z > 0)
            def _():
                start(old_msg, slot, 0, half)

            start(old_msg, slot, 2, half)

    comps = ((compk_vm, compk), (compv_vm, compv))

    def comp_msg(d, part, who):
        return pltpu.make_async_remote_copy(
            src_ref=comps[part][0],
            dst_ref=comps[part][1].at[who],
            send_sem=comp_send.at[d - 1, part],
            recv_sem=comp_recv.at[who, part],
            device_id={"seq": lax.rem(me + d, n_seq)},
            device_id_type=MESH,
        )

    def comp_keep(part):
        return pltpu.make_async_copy(comps[part][0], comps[part][1].at[me], own_sem.at[part])

    def spread_tokens():
        tail = SEL_BLOCK - CMP_STRIDE

        @pl.when(me > 0)
        def _():
            recv(old_msg, me - 1, 1)
            block = me * per - 1
            k_ext[0:CMP_STRIDE, 0:vw] = kh[block, tail:SEL_BLOCK]
            k_ext[0:CMP_STRIDE, vw:width] = kl[block, tail - half_block : half_block, low:]
            v_ext[0:CMP_STRIDE, :] = v[block, tail:SEL_BLOCK]

        @pl.when(me == 0)
        def _():
            k_ext[0:CMP_STRIDE, :] = jnp.zeros((CMP_STRIDE, width), jnp.bfloat16)
            v_ext[0:CMP_STRIDE, :] = jnp.zeros((CMP_STRIDE, vw), jnp.bfloat16)

        for lhs, ext in ((lhs_k, k_ext), (lhs_v, v_ext)):
            spread = jnp.dot(perm[...], ext[...], preferred_element_type=jnp.float32)
            spread = spread.astype(jnp.bfloat16)
            each = ext.shape[1]
            for p in range(CMP_STRIDE):
                lhs[:, p * each : (p + 1) * each] = spread[p * pad : (p + 1) * pad]

    def pass_weights():
        for d in range(1, n_kv):
            who = lax.rem(group + n_kv - d, n_kv)
            for part in range(2):
                w_arrived(who, core, part).wait_recv()
                w_arrived(who, core, part).start()

    def compress():
        for d in range(1, n_kv):
            who = lax.rem(group + n_kv - d, n_kv)
            for part in range(2):
                w_arrived(who, 1 - core, part).wait_recv()
        for lhs, w, held, dims in (
            (lhs_k, wk_all, compk_vm, (((1,), (1,)), ((), ()))),
            (lhs_v, wv_all, compv_vm, (((1,), (0,)), ((), ()))),
        ):
            pieces = n_kv * CORES // 2
            depth = lhs.shape[1] // pieces
            sums = []
            for side in range(2):
                total = None
                for n in range(pieces):
                    at = side * pieces + n
                    term = lax.dot_general(
                        lhs[:, n * depth : (n + 1) * depth],
                        w[at // CORES, at % CORES],
                        dims,
                        preferred_element_type=jnp.float32,
                    )
                    total = term if total is None else total + term
                sums.append(total)
            held[...] = (sums[0][0:chunks] + sums[1][1 : chunks + 1]).astype(jnp.bfloat16)
        for part in range(2):
            comp_keep(part).start()
        for d in range(1, n_seq):
            for part in range(2):
                comp_msg(d, part, me).start()

    def attend(rows, keys, values, allowed):
        s = lax.dot_general(
            rows, keys, (((1,), (1,)), ((), ())), preferred_element_type=jnp.float32
        )
        if allowed is not None:
            s = jnp.where(allowed, s, MASKED)
        top = jnp.max(s, axis=-1, keepdims=True)
        w = jnp.exp2((s - top) * factor)
        total = jnp.sum(w, axis=-1, keepdims=True)
        o = jnp.dot(w.astype(jnp.bfloat16), values, preferred_element_type=jnp.float32)
        return o / total

    def gated(branch, t, o, emit):
        g = gates_vm[pl.ds(pl.multiple_of(t * count, count), count), :]
        for h in range(heads):
            a = slice(h * tile, (h + 1) * tile)
            at = branch * heads + h
            emit(h, pl.ds(pl.multiple_of(t * count + h * tile, tile), tile), g[a, at : at + 1] * o[a])

    def rows_of(t):
        return rows_vm[pl.ds(pl.multiple_of(t * count, count), count), :]

    def compressed():
        for part in range(2):
            comp_keep(part).wait()
        for d in range(1, n_seq):
            who = lax.rem(me + d, n_seq)
            for part in range(2):
                comp_msg(d, part, who).wait_recv()
        total = n_seq * chunks
        ok = lax.broadcasted_iota(jnp.int32, (count, total), 1) > 0

        @pl.loop(0, tiles)
        def _(t):
            o = attend(
                rows_of(t),
                compk[...].reshape(total, width),
                compv[...].reshape(total, vw),
                ok,
            )

            def emit(h, at, x):
                acc[at, :] = x

            gated(0, t, o, emit)

    def put(dk, dv, at, khv, vv, klv):
        dk[pl.ds(at, SEL_BLOCK), 0:vw] = khv
        dk[pl.ds(at, half_block), vw:width] = klv[:, 0:low]
        dk[pl.ds(at + half_block, half_block), vw:width] = klv[:, low : 2 * low]
        dv[pl.ds(at, SEL_BLOCK), :] = vv

    def window():
        @pl.when(core == 0)
        def _():
            recv(old_msg, n_seq - 1, 1)

        for d in range(0, min(hops, chips - 1) + 1):

            @pl.when(z >= d)
            def _():
                recv(new_msg, (z - d) * CORES + 1 - core, 0)

        for i in range(lookback + 1):
            chunk = me + i
            for b in range(new_per):
                at = (i * new_per + b) * SEL_BLOCK

                @pl.when(chunk < lookback)
                def _():
                    block = n_seq * per - lookback * new_per + chunk * new_per + b
                    put(win_k, win_v, at, kh[block], v[block], kl[block])

                @pl.when(chunk >= lookback)
                def _():
                    block = (chunk - lookback) * new_per + b
                    put(win_k, win_v, at, nkh[block], nv[block], nkl[block])

        span = WINDOW + tile
        diff = lax.broadcasted_iota(jnp.int32, (count, span), 1) - lax.rem(
            lax.broadcasted_iota(jnp.int32, (count, span), 0), tile
        )
        ok = (diff > 0) & (diff <= WINDOW)

        @pl.loop(0, tiles)
        def _(t):
            off = pl.multiple_of(t * tile, tile)
            o = attend(rows_of(t), win_k[pl.ds(off, span), :], win_v[pl.ds(off, span), :], ok)

            def emit(h, at, x):
                acc[at, :] += x

            gated(2, t, o, emit)

    def selected():
        picks = sel.shape[1]

        @pl.loop(0, tiles)
        def _(t):
            for n in range(picks):
                block = sel[t, n]
                put(sel_k, sel_v, n * SEL_BLOCK, kh[block], v[block], kl[block])
            o = attend(rows_of(t), sel_k[...], sel_v[...], None)

            def emit(h, at, x):
                to = pl.ds(pl.multiple_of(t * tile, tile), tile)
                out[to, h * vw : (h + 1) * vw] = (acc[at, :] + x).astype(out.dtype)

            gated(1, t, o, emit)

    relay(1, 1)
    relay(1, 0)
    spread_tokens()
    pass_weights()
    for d in range(2, chips - 1):
        relay(d, 1)
    compress()
    for d in range(2, chips - 1):
        relay(d, 0)
    compressed()
    relay(chips - 1, 1)
    window()
    relay(chips - 1, 0)

    for zz in range(chips):
        slot = zz * CORES + 1 - core
        recv(old_msg, slot, 0)
        early = slot == me - 1
        if zz == chips - 1:
            early = early | (core == 0)

        @pl.when(jnp.logical_not(early))
        def _():
            recv(old_msg, slot, 1)

    selected()

    for d in range(1, n_kv):
        for part in range(2):
            w_msg(d, part).wait_send()
            w_arrived(lax.rem(group + n_kv - d, n_kv), core, part).wait_send()
    for d in range(1, n_seq):
        for part in range(2):
            comp_msg(d, part, me).wait_send()

    def all_sent(slot, ways):
        for way in ways:
            for half in range(2):
                sent(old_msg, slot, way, half)

    @pl.when(z < chips - 1)
    def _():
        sent(new_msg, me, 1, 0)
        all_sent(me, (1,))

    @pl.when(z > 0)
    def _():
        all_sent(me, (0,))

    sent(new_msg, me, 2, 0)
    all_sent(me, (2,))
    for d in range(1, chips):

        @pl.when(z >= d)
        def _():
            slot = me - CORES * d
            if d <= hops:
                sent(new_msg, slot, 2, 0)

                if d < hops:

                    @pl.when(z < chips - 1)
                    def _():
                        sent(new_msg, slot, 1, 0)

            all_sent(slot, (2,))

            @pl.when(z < chips - 1)
            def _():
                all_sent(slot, (1,))

        @pl.when(z + d < chips)
        def _():
            slot = me + CORES * d
            all_sent(slot, (2,))

            @pl.when(z > 0)
            def _():
                all_sent(slot, (0,))


def shards_gathered(q, ck, cv, ik, iv, wk, wv, sel, gw):
    n_seq, n_kv = lax.axis_size("seq"), lax.axis_size("kv")
    heads, width, branches = gw.shape
    vw = cv.shape[1]
    cache, fresh = ck.shape[0], ik.shape[0]
    tiles, picks = sel.shape[0], sel.shape[-1]
    chunks = cache // CMP_STRIDE
    pad = chunks + CMP_STRIDE
    per, new_per = cache // SEL_BLOCK, fresh // SEL_BLOCK
    tile_rows = heads * fresh
    bf = jnp.bfloat16
    any_spec = pl.BlockSpec(memory_space=pl.ANY)
    half_k, half_v = wk.shape[0] // CORES, wv.shape[0] // CORES

    def held(*shape):
        return pltpu.VMEM(shape, bf)

    dma = pltpu.SemaphoreType.DMA
    return pl.pallas_call(
        functools.partial(fused_kernel, n_seq, n_kv, tiles),
        out_shape=jax.ShapeDtypeStruct((fresh, heads * vw), bf),
        in_specs=[pl.BlockSpec(memory_space=pltpu.SMEM)] + [any_spec] * 8,
        out_specs=pl.BlockSpec(memory_space=pltpu.VMEM),
        scratch_shapes=[
            held(*q.shape),
            held(width, cache),
            held(width, fresh),
            held(heads * branches, width),
            held(n_seq * per, SEL_BLOCK, vw),
            held(n_seq * per, SEL_BLOCK, vw),
            held(n_seq * per, SEL_BLOCK // 2, vw),
            held(n_seq * new_per, SEL_BLOCK, vw),
            held(n_seq * new_per, SEL_BLOCK, vw),
            held(n_seq * new_per, SEL_BLOCK // 2, vw),
            held(cache + CMP_STRIDE, width),
            held(cache + CMP_STRIDE, vw),
            held(CMP_STRIDE * pad, cache + CMP_STRIDE),
            held(pad, CMP_STRIDE * width),
            held(pad, CMP_STRIDE * vw),
            held(n_kv, CORES, width, half_k),
            held(n_kv, CORES, half_v, vw),
            held(chunks, width),
            held(chunks, vw),
            held(n_seq, chunks, width),
            held(n_seq, chunks, vw),
            held(tile_rows, width),
            pltpu.VMEM((tile_rows, heads * branches), jnp.float32),
            pltpu.VMEM((tile_rows, vw), jnp.float32),
            held(fresh + WINDOW, width),
            held(fresh + WINDOW, vw),
            held(picks * SEL_BLOCK, width),
            held(picks * SEL_BLOCK, vw),
            dma((6 + 2 * CORES,)),
            dma((2,)),
            dma((3, n_seq, 3, 2)),
            dma((n_seq, 3, 2)),
            dma((3, n_seq, 3)),
            dma((n_seq, 3)),
            dma((2 * (n_kv - 1), 2)),
            dma((n_kv, CORES, 2)),
            dma((n_seq - 1, 2)),
            dma((n_seq, 2)),
        ],
        compiler_params=pltpu.CompilerParams(
            collective_id=0, has_side_effects=True, vmem_limit_bytes=60 << 20
        ),
    )(
        sel.reshape(tiles, picks),
        q,
        ck.T,
        cv.reshape(per, SEL_BLOCK, vw),
        ik.T,
        iv.reshape(new_per, SEL_BLOCK, vw),
        wk.T,
        wv,
        jnp.transpose(gw, (2, 0, 1)).reshape(heads * branches, width),
    )


GATHER_BYTES = 1 << 24


def shards(queries, cache_keys, cache_values, *rest):
    ranks = lax.axis_size("seq")
    size = ranks * 2 * (cache_keys.size + cache_values.size)
    form = shards_gathered if size <= GATHER_BYTES else shards_by_request
    return form(queries, cache_keys, cache_values, *rest)


def solution(mesh):
    placed = (
        P("seq", "kv"),
        P("seq", "kv"),
        P("seq", "kv"),
        P("seq", "kv"),
        P("seq", "kv"),
        P("kv", None),
        P("kv", None),
        P("seq", "kv", None),
        P("kv", None, None),
    )
    return jax.shard_map(
        shards, mesh=mesh, in_specs=placed, out_specs=P("seq", "kv"), check_vma=False
    )
```

```python
import functools

import jax
import jax.numpy as jnp
from jax import lax
from jax.experimental import pallas as pl
from jax.experimental.pallas import tpu as pltpu
from jax.sharding import PartitionSpec as P

CMP_STRIDE = 16
SEL_BLOCK = 64
WINDOW = 512


MASKED = -1e30


def passed_along(block, axis, distance):
    devices = range(lax.axis_size(axis))
    route = [((i - distance) % len(devices), i) for i in devices]
    return lax.ppermute(block, axis, route)


def from_behind(x, axis, by):
    peers = lax.axis_size(axis)
    pairs = [(i, i + by) for i in range(peers) if 0 <= i + by < peers]
    return lax.ppermute(x, axis, pairs)


def pack_rows(keys, values):
    return jnp.concatenate([keys.reshape(-1), values.reshape(-1)])


def unpack_rows(flat, count, key_width, value_width):
    keys = flat[: count * key_width].reshape(count, key_width)
    values = flat[count * key_width : count * (key_width + value_width)].reshape(count, value_width)
    return (keys, values)


def finish_rows(scores, values):
    top = jnp.max(scores, axis=-1, keepdims=True)
    weights = jnp.exp(scores - top)
    total = jnp.sum(weights, axis=-1, keepdims=True)
    mixed = jnp.matmul(weights.astype(jnp.bfloat16), values, preferred_element_type=jnp.float32)
    return mixed / total


def shards_by_request(
    queries,
    cache_keys,
    cache_values,
    incoming_keys,
    new_values,
    comp_key_weight,
    comp_value_weight,
    select_blocks,
    gate_weight,
):
    heads, key_width, _ = gate_weight.shape
    value_width = cache_values.shape[1]
    query_count = queries.shape[0]
    cache_count = cache_keys.shape[0]
    ranks = lax.axis_size("seq")
    place = lax.axis_index("seq")
    scale = key_width ** (-0.5)
    rows = queries.reshape(query_count * heads, key_width)
    row_total = rows.shape[0]
    stretch_pos = place * query_count + jnp.arange(query_count, dtype=jnp.int32)
    lookback_length = -(-WINDOW // query_count)
    weight_keys, weight_values = (
        lax.all_gather(comp_key_weight, "kv", axis=0, tiled=True),
        lax.all_gather(comp_value_weight, "kv", axis=0, tiled=True),
    )
    tail_pack = pack_rows(cache_keys[cache_count - WINDOW :], cache_values[cache_count - WINDOW :])
    moved_tail = passed_along(tail_pack, "seq", 1)
    before_keys, before_values = unpack_rows(moved_tail, WINDOW, key_width, value_width)
    edge_keys = before_keys[WINDOW - CMP_STRIDE :]
    edge_values = before_values[WINDOW - CMP_STRIDE :]
    held_tail = jnp.where(place == 0, moved_tail, jnp.zeros_like(moved_tail))
    tail_size = held_tail.shape[0]
    tail_flat = held_tail
    near_keys = []
    near_values = []
    nearby_positions = []
    near_valid = []
    own = pack_rows(incoming_keys, new_values)
    own_size = own.shape[0]
    for back in range(lookback_length, 0, -1):
        moved = from_behind(jnp.concatenate([own, held_tail]), "seq", back)
        got_keys, got_values = unpack_rows(moved, query_count, key_width, value_width)
        tail_flat = jnp.where(place == back, moved[own_size : own_size + tail_size], tail_flat)
        near_keys.append(got_keys)
        near_values.append(got_values)
        nearby_positions.append(
            (place - back) * query_count + jnp.arange(query_count, dtype=jnp.int32)
        )
        near_valid.append(jnp.broadcast_to(place >= back, (query_count,)))
    tail_keys, tail_values = unpack_rows(tail_flat, WINDOW, key_width, value_width)
    near_keys.append(tail_keys)
    near_values.append(tail_values)
    nearby_positions.append(jnp.arange(WINDOW, dtype=jnp.int32) - WINDOW)
    near_valid.append(jnp.ones((WINDOW,), dtype=bool))
    near_keys.append(incoming_keys)
    near_values.append(new_values)
    nearby_positions.append(stretch_pos)
    near_valid.append(jnp.ones((query_count,), dtype=bool))
    half_keys = CMP_STRIDE * key_width
    half_values = CMP_STRIDE * value_width
    lead_keys = jnp.concatenate([edge_keys, cache_keys[: cache_count - CMP_STRIDE]]).reshape(
        -1, half_keys
    )
    lead_values = jnp.concatenate([edge_values, cache_values[: cache_count - CMP_STRIDE]]).reshape(
        -1, half_values
    )
    comp_keys = (
        jnp.dot(lead_keys, weight_keys[:half_keys], preferred_element_type=jnp.float32)
        + jnp.dot(
            cache_keys.reshape(-1, half_keys),
            weight_keys[half_keys:],
            preferred_element_type=jnp.float32,
        )
    ).astype(jnp.bfloat16)
    comp_values = (
        jnp.dot(lead_values, weight_values[:half_values], preferred_element_type=jnp.float32)
        + jnp.dot(
            cache_values.reshape(-1, half_values),
            weight_values[half_values:],
            preferred_element_type=jnp.float32,
        )
    ).astype(jnp.bfloat16)
    start = jnp.int32(0)
    top = jnp.full((row_total,), MASKED, jnp.float32)
    total = jnp.zeros((row_total,), jnp.float32)
    summed = jnp.zeros((row_total, value_width), jnp.float32)
    keys = lax.all_gather(comp_keys, "seq", axis=0, tiled=True)
    values = lax.all_gather(comp_values, "seq", axis=0, tiled=True)
    length = keys.shape[0]
    block = length
    for size in (1024, 512, 256, 128):
        if length % size == 0:
            block = size
            break
    for index in range(length // block):
        key_block = keys[index * block : (index + 1) * block]
        value_block = values[index * block : (index + 1) * block]
        scores = (
            jnp.einsum("rd,kd->rk", rows, key_block, preferred_element_type=jnp.float32) * scale
        )
        key_at = start + index * block + jnp.arange(block, dtype=jnp.int32)
        scores = jnp.where(key_at[None, :] > 0, scores, MASKED)
        newtop = jnp.maximum(top, jnp.max(scores, axis=1))
        factor = jnp.exp(top - newtop)
        weights = jnp.exp(scores - newtop[:, None])
        total = total * factor + jnp.sum(weights, axis=1)
        summed = summed * factor[:, None] + jnp.dot(
            weights.astype(jnp.bfloat16), value_block, preferred_element_type=jnp.float32
        )
        top = newtop
    top, total, summed = (top, total, summed)
    compressed_out = summed / total[:, None]
    chosen = select_blocks.reshape(-1)
    shard_blocks = cache_count // SEL_BLOCK
    capacity = max(2, 2 * chosen.shape[0] // ranks)
    owner = chosen // shard_blocks
    local = chosen - owner * shard_blocks
    onehot = (owner[:, None] == jnp.arange(ranks, dtype=jnp.int32)[None, :]).astype(jnp.int32)
    position = jnp.sum((jnp.cumsum(onehot, axis=0) - 1) * onehot, axis=1)
    request = jnp.full((ranks, capacity), -1, jnp.int32).at[owner, position].set(local)
    key_blocks = cache_keys.reshape(shard_blocks, SEL_BLOCK, key_width)
    value_block_list = cache_values.reshape(shard_blocks, SEL_BLOCK, value_width)
    safe = jnp.clip(
        lax.all_to_all(request, "seq", split_axis=0, concat_axis=0, tiled=True), 0, shard_blocks - 1
    )
    got_keys = lax.all_to_all(key_blocks[safe], "seq", split_axis=0, concat_axis=0, tiled=True)
    got_values = lax.all_to_all(
        value_block_list[safe], "seq", split_axis=0, concat_axis=0, tiled=True
    )
    where_at = owner * capacity + position
    tile_count = select_blocks.shape[0]
    gathered_keys = got_keys.reshape(ranks * capacity, SEL_BLOCK, key_width)[where_at]
    picked_values = got_values.reshape(ranks * capacity, SEL_BLOCK, value_width)[where_at]
    gathered_keys, picked_values = (
        gathered_keys.reshape(tile_count, -1, key_width),
        picked_values.reshape(tile_count, -1, value_width),
    )
    tile_count = gathered_keys.shape[0]
    tile_row_count = rows.reshape(tile_count, -1, key_width)
    tile_scores = (
        jnp.einsum(
            "izu,ixu->izx", tile_row_count, gathered_keys, preferred_element_type=jnp.float32
        )
        * scale
    )
    selected_out = finish_rows(tile_scores, picked_values).reshape(row_total, value_width)
    context_keys = jnp.concatenate(near_keys)
    context_values = jnp.concatenate(near_values)
    context_positions = jnp.concatenate(nearby_positions)
    context_valid = jnp.concatenate(near_valid)
    sliding_scores = (
        jnp.einsum("rd,kd->rk", rows, context_keys, preferred_element_type=jnp.float32) * scale
    )
    allowed = (
        context_valid[None, :]
        & (context_positions[None, :] <= stretch_pos[:, None])
        & (context_positions[None, :] > stretch_pos[:, None] - WINDOW)
    )
    sliding_scores = jnp.where(
        allowed[:, None, :], sliding_scores.reshape(query_count, heads, -1), MASKED
    )
    window_out = finish_rows(sliding_scores.reshape(row_total, -1), context_values)
    logits = jnp.einsum(
        "thd,hdb->thb",
        queries.reshape(query_count, heads, key_width),
        gate_weight,
        preferred_element_type=jnp.float32,
    )
    gates = jax.nn.sigmoid(logits)
    mixed = (
        gates[:, :, 0:1] * compressed_out.reshape(query_count, heads, value_width)
        + gates[:, :, 1:2] * selected_out.reshape(query_count, heads, value_width)
        + gates[:, :, 2:3] * window_out.reshape(query_count, heads, value_width)
    )
    return mixed.astype(jnp.bfloat16).reshape(query_count, heads * value_width)


CORES = 2
PIECES = 4
LOG2E = 1.4426950408889634
MESH = pl.DeviceIdType.MESH


def fused_kernel(
    n_seq,
    n_kv,
    tiles,
    sel,
    q,
    ckt,
    cv,
    ikt,
    iv,
    wkt,
    wv,
    gw,
    out,
    q_vm,
    ckt_vm,
    ikt_vm,
    gw_vm,
    kh,
    v,
    kl,
    nkh,
    nv,
    nkl,
    k_ext,
    v_ext,
    perm,
    lhs_k,
    lhs_v,
    wk_all,
    wv_all,
    comp_vm,
    comp_all,
    compk,
    compv,
    rows_vm,
    gates_vm,
    acc,
    win_k,
    win_v,
    sel_k,
    sel_v,
    local_sem,
    own_sem,
    kv_send,
    kv_recv,
    new_send,
    new_recv,
    w_send,
    w_recv,
    comp_send,
    comp_recv,
):
    me = lax.axis_index("seq")
    group = lax.axis_index("kv")
    z = me // CORES
    core = lax.rem(me, CORES)
    chips = n_seq // CORES
    mate = z * CORES + 1 - core
    left = lax.rem(me - CORES + n_seq, n_seq)
    right = lax.rem(me + CORES, n_seq)
    route = (left, right, mate)
    width, cache = ckt.shape
    fresh = ikt.shape[1]
    vw = v.shape[2]
    low = width - vw
    per = cache // SEL_BLOCK
    new_per = fresh // SEL_BLOCK
    half_block = SEL_BLOCK // 2
    heads = q.shape[1] // width
    tile = fresh // tiles
    count = heads * tile
    lookback = WINDOW // fresh
    hops = -(-lookback // CORES)
    chunks = cache // CMP_STRIDE
    pad = chunks + CMP_STRIDE
    factor = width**-0.5 * LOG2E

    barrier = pltpu.get_barrier_semaphore()
    for d in range(1, n_seq):
        pl.semaphore_signal(
            barrier, inc=1, device_id={"seq": lax.rem(me + d, n_seq)}, device_id_type=MESH
        )
    for d in range(1, n_kv):
        pl.semaphore_signal(
            barrier, inc=1, device_id={"kv": lax.rem(group + d, n_kv)}, device_id_type=MESH
        )

    half_k = wkt.shape[1] // CORES
    half_v = wv.shape[0] // CORES
    loads = [
        (cv, v.at[pl.ds(me * per, per)]),
        (iv, nv.at[pl.ds(me * new_per, new_per)]),
        (ckt, ckt_vm),
        (ikt, ikt_vm),
        (q, q_vm),
        (gw, gw_vm),
    ]
    for half in range(CORES):
        loads.append((wkt.at[:, pl.ds(half * half_k, half_k)], wk_all.at[group, half]))
        loads.append((wv.at[pl.ds(half * half_v, half_v)], wv_all.at[group, half]))
    load_copies = [pltpu.make_async_copy(a, b, local_sem.at[n]) for n, (a, b) in enumerate(loads)]
    for copy in load_copies:
        copy.start()

    old = (v, kh, kl)
    new = (nv, nkh, nkl)

    def pieces_of(half):
        return range(PIECES // 2 * half, PIECES // 2 * (half + 1))[::-1]

    def old_msg(slot, way, part, piece):
        size = per // PIECES
        ref = old[part].at[pl.ds(slot * per + piece * size, size)]
        return pltpu.make_async_remote_copy(
            src_ref=ref,
            dst_ref=ref,
            send_sem=kv_send.at[way, slot, part, piece],
            recv_sem=kv_recv.at[slot, part, piece],
            device_id={"seq": route[way]},
            device_id_type=MESH,
        )

    def new_msg(slot, way, part, half):
        ref = new[part].at[pl.ds(slot * new_per, new_per)]
        return pltpu.make_async_remote_copy(
            src_ref=ref,
            dst_ref=ref,
            send_sem=new_send.at[way, slot, part],
            recv_sem=new_recv.at[slot, part],
            device_id={"seq": route[way]},
            device_id_type=MESH,
        )

    def start(make, slot, way, half, parts=range(3)):
        for part in parts:
            make(slot, way, part, half).start()

    def recv(make, slot, half):
        for part in range(3):
            make(slot, 2, part, half).wait_recv()

    def sent(make, slot, way, half):
        for part in range(3):
            make(slot, way, part, half).wait_send()

    def start_own(parts):
        for half in range(PIECES)[::-1]:

            @pl.when(z < chips - 1)
            def _():
                start(old_msg, me, 1, half, parts)

            @pl.when(z > 0)
            def _():
                start(old_msg, me, 0, half, parts)

            start(old_msg, me, 2, half, parts)

    w_all = (wk_all, wv_all)
    w_own = (
        wkt.at[:, pl.ds(pl.multiple_of(core * half_k, half_k), half_k)],
        wv.at[pl.ds(pl.multiple_of(core * half_v, half_v), half_v)],
    )

    def w_msg(d, part):
        return pltpu.make_async_remote_copy(
            src_ref=w_own[part],
            dst_ref=w_all[part].at[group, core],
            send_sem=w_send.at[d - 1, part],
            recv_sem=w_recv.at[group, core, part],
            device_id={"kv": lax.rem(group + d, n_kv)},
            device_id_type=MESH,
        )

    def w_arrived(who, half, part):
        return pltpu.make_async_remote_copy(
            src_ref=w_all[part].at[who, half],
            dst_ref=w_all[part].at[who, half],
            send_sem=w_send.at[n_kv - 1 + lax.rem(who - group + n_kv, n_kv) - 1, part],
            recv_sem=w_recv.at[who, half, part],
            device_id={"seq": mate},
            device_id_type=MESH,
        )

    load_copies[0].wait()
    load_copies[1].wait()
    pl.semaphore_wait(barrier, n_seq - 1 + n_kv - 1)
    start_own((0,))
    for d in range(1, n_kv):
        for part in range(2):
            w_msg(d, part).start()

    def pack(keys, blocks, hi, lo, at):
        hi[pl.ds(at, blocks)] = keys[:, 0:vw].reshape(blocks, SEL_BLOCK, vw)
        part = keys[:, vw:width].reshape(blocks, 2, half_block, low)
        lo[pl.ds(at, blocks)] = jnp.concatenate([part[:, 0], part[:, 1]], axis=-1)

    load_copies[2].wait()
    keys = ckt_vm[...].T
    pack(keys, per, kh, kl, me * per)
    k_ext[CMP_STRIDE:, :] = keys
    load_copies[3].wait()
    pack(ikt_vm[...].T, new_per, nkh, nkl, me * new_per)
    v_ext[CMP_STRIDE:, :] = v[pl.ds(me * per, per)].reshape(cache, vw)
    for copy in load_copies[4:]:
        copy.wait()

    @pl.when(z < chips - 1)
    def _():
        start(new_msg, me, 1, 0)

    start_own((1, 2))
    start(new_msg, me, 2, 0)

    @pl.loop(0, tiles)
    def _(t):
        part = q_vm[pl.ds(pl.multiple_of(t * tile, tile), tile), :]
        for h in range(heads):
            at = pl.multiple_of(t * count + h * tile, tile)
            rows_vm[pl.ds(at, tile), :] = part[:, h * width : (h + 1) * width]

    logits = lax.dot_general(
        rows_vm[...], gw_vm[...], (((1,), (1,)), ((), ())), preferred_element_type=jnp.float32
    )
    gates_vm[...] = jax.nn.sigmoid(logits)
    lag = lax.broadcasted_iota(jnp.int32, (pad, cache + CMP_STRIDE), 1)
    lag = lag - CMP_STRIDE * lax.broadcasted_iota(jnp.int32, lag.shape, 0)

    @pl.loop(0, CMP_STRIDE)
    def _(p):
        at = pl.multiple_of(p * pad, CMP_STRIDE)
        perm[pl.ds(at, pad), :] = jnp.where(lag == p, 1.0, 0.0).astype(jnp.bfloat16)

    for d in range(1, min(hops, chips - 1) + 1):

        @pl.when(z >= d)
        def _():
            slot = me - CORES * d
            recv(new_msg, slot, 0)
            if d < hops:

                @pl.when(z < chips - 1)
                def _():
                    start(new_msg, slot, 1, 0)

            start(new_msg, slot, 2, 0)

    def relay(d, side):
        for piece in pieces_of(side):
            relay_piece(d, piece)

    def recv_side(slot, side):
        for piece in pieces_of(side):
            recv(old_msg, slot, piece)

    def relay_piece(d, half):
        @pl.when(z >= d)
        def _():
            slot = me - CORES * d
            recv(old_msg, slot, half)

            @pl.when(z < chips - 1)
            def _():
                start(old_msg, slot, 1, half)

            start(old_msg, slot, 2, half)

        @pl.when(z + d < chips)
        def _():
            slot = me + CORES * d
            recv(old_msg, slot, half)

            @pl.when(z > 0)
            def _():
                start(old_msg, slot, 0, half)

            start(old_msg, slot, 2, half)

    def comp_send_own(d):
        to = lax.rem(me + CORES * d, n_seq) if d else mate
        return pltpu.make_async_remote_copy(
            src_ref=comp_vm,
            dst_ref=comp_all.at[me],
            send_sem=comp_send.at[d],
            recv_sem=comp_recv.at[me],
            device_id={"seq": to},
            device_id_type=MESH,
        )

    def comp_pass(d):
        who = lax.rem(me + CORES * d, n_seq)
        return pltpu.make_async_remote_copy(
            src_ref=comp_all.at[who],
            dst_ref=comp_all.at[who],
            send_sem=comp_send.at[chips + d - 1],
            recv_sem=comp_recv.at[who],
            device_id={"seq": mate},
            device_id_type=MESH,
        )

    def comp_take(who):
        return pltpu.make_async_remote_copy(
            src_ref=comp_all.at[who],
            dst_ref=comp_all.at[who],
            send_sem=comp_send.at[0],
            recv_sem=comp_recv.at[who],
            device_id={"seq": mate},
            device_id_type=MESH,
        )

    comp_keep = pltpu.make_async_copy(comp_vm, comp_all.at[me], own_sem)

    def spread_tokens():
        tail = SEL_BLOCK - CMP_STRIDE

        @pl.when(me > 0)
        def _():
            recv_side(me - 1, 1)
            block = me * per - 1
            k_ext[0:CMP_STRIDE, 0:vw] = kh[block, tail:SEL_BLOCK]
            k_ext[0:CMP_STRIDE, vw:width] = kl[block, tail - half_block : half_block, low:]
            v_ext[0:CMP_STRIDE, :] = v[block, tail:SEL_BLOCK]

        @pl.when(me == 0)
        def _():
            k_ext[0:CMP_STRIDE, :] = jnp.zeros((CMP_STRIDE, width), jnp.bfloat16)
            v_ext[0:CMP_STRIDE, :] = jnp.zeros((CMP_STRIDE, vw), jnp.bfloat16)

        for lhs, ext in ((lhs_k, k_ext), (lhs_v, v_ext)):
            spread = jnp.dot(perm[...], ext[...], preferred_element_type=jnp.float32)
            spread = spread.astype(jnp.bfloat16)
            each = ext.shape[1]
            for p in range(CMP_STRIDE):
                lhs[:, p * each : (p + 1) * each] = spread[p * pad : (p + 1) * pad]

    def pass_weights():
        for d in range(1, n_kv):
            who = lax.rem(group + n_kv - d, n_kv)
            for part in range(2):
                w_arrived(who, core, part).wait_recv()
                w_arrived(who, core, part).start()

    def compress():
        for d in range(1, n_kv):
            who = lax.rem(group + n_kv - d, n_kv)
            for part in range(2):
                w_arrived(who, 1 - core, part).wait_recv()
        results = []
        for lhs, w, dims in (
            (lhs_k, wk_all, (((1,), (1,)), ((), ()))),
            (lhs_v, wv_all, (((1,), (0,)), ((), ()))),
        ):
            pieces = n_kv * CORES // 2
            depth = lhs.shape[1] // pieces
            sums = []
            for side in range(2):
                total = None
                for n in range(pieces):
                    at = side * pieces + n
                    term = lax.dot_general(
                        lhs[:, n * depth : (n + 1) * depth],
                        w[at // CORES, at % CORES],
                        dims,
                        preferred_element_type=jnp.float32,
                    )
                    total = term if total is None else total + term
                sums.append(total)
            results.append((sums[0][0:chunks] + sums[1][1 : chunks + 1]).astype(jnp.bfloat16))
        made, made_v = results
        comp_vm[0:chunks, :] = made[:, 0:vw]
        comp_vm[chunks : 2 * chunks, :] = made_v
        comp_vm[2 * chunks :, :] = jnp.concatenate(
            [made[0 : chunks // 2, vw:width], made[chunks // 2 :, vw:width]], axis=-1
        )
        for d in range(1, chips):
            comp_send_own(d).start()
        comp_send_own(0).start()
        comp_keep.start()

    def attend(rows, keys, values, allowed):
        s = lax.dot_general(
            rows, keys, (((1,), (1,)), ((), ())), preferred_element_type=jnp.float32
        )
        if allowed is not None:
            s = jnp.where(allowed, s, MASKED)
        top = jnp.max(s, axis=-1, keepdims=True)
        w = jnp.exp2((s - top) * factor)
        total = jnp.sum(w, axis=-1, keepdims=True)
        o = jnp.dot(w.astype(jnp.bfloat16), values, preferred_element_type=jnp.float32)
        return o / total

    def gated(branch, t, o, emit):
        g = gates_vm[pl.ds(pl.multiple_of(t * count, count), count), :]
        for h in range(heads):
            a = slice(h * tile, (h + 1) * tile)
            at = branch * heads + h
            emit(h, pl.ds(pl.multiple_of(t * count + h * tile, tile), tile), g[a, at : at + 1] * o[a])

    def rows_of(t):
        return rows_vm[pl.ds(pl.multiple_of(t * count, count), count), :]

    def compressed():
        comp_keep.wait()
        for d in range(1, chips):
            comp_pass(d).wait_recv()
            comp_pass(d).start()
        for zz in range(chips):
            comp_take(zz * CORES + 1 - core).wait_recv()
        total = n_seq * chunks
        for slot in range(n_seq):
            at, mid = slot * chunks, slot * chunks + chunks // 2
            compk[at : at + chunks, 0:vw] = comp_all[slot, 0:chunks]
            compk[at:mid, vw:width] = comp_all[slot, 2 * chunks :, 0:low]
            compk[mid : at + chunks, vw:width] = comp_all[slot, 2 * chunks :, low : 2 * low]
            compv[at : at + chunks, :] = comp_all[slot, chunks : 2 * chunks]
        ok = lax.broadcasted_iota(jnp.int32, (count, total), 1) > 0

        @pl.loop(0, tiles)
        def _(t):
            o = attend(
                rows_of(t),
                compk[...],
                compv[...],
                ok,
            )

            def emit(h, at, x):
                acc[at, :] = x

            gated(0, t, o, emit)

    def put(dk, dv, at, khv, vv, klv):
        dk[pl.ds(at, SEL_BLOCK), 0:vw] = khv
        dk[pl.ds(at, half_block), vw:width] = klv[:, 0:low]
        dk[pl.ds(at + half_block, half_block), vw:width] = klv[:, low : 2 * low]
        dv[pl.ds(at, SEL_BLOCK), :] = vv

    def window():
        @pl.when(core == 0)
        def _():
            recv_side(n_seq - 1, 1)

        for d in range(0, min(hops, chips - 1) + 1):

            @pl.when(z >= d)
            def _():
                recv(new_msg, (z - d) * CORES + 1 - core, 0)

        for i in range(lookback + 1):
            chunk = me + i
            for b in range(new_per):
                at = (i * new_per + b) * SEL_BLOCK

                @pl.when(chunk < lookback)
                def _():
                    block = n_seq * per - lookback * new_per + chunk * new_per + b
                    put(win_k, win_v, at, kh[block], v[block], kl[block])

                @pl.when(chunk >= lookback)
                def _():
                    block = (chunk - lookback) * new_per + b
                    put(win_k, win_v, at, nkh[block], nv[block], nkl[block])

        span = WINDOW + tile
        diff = lax.broadcasted_iota(jnp.int32, (count, span), 1) - lax.rem(
            lax.broadcasted_iota(jnp.int32, (count, span), 0), tile
        )
        ok = (diff > 0) & (diff <= WINDOW)

        @pl.loop(0, tiles)
        def _(t):
            off = pl.multiple_of(t * tile, tile)
            o = attend(rows_of(t), win_k[pl.ds(off, span), :], win_v[pl.ds(off, span), :], ok)

            def emit(h, at, x):
                acc[at, :] += x

            gated(2, t, o, emit)

    def selected():
        picks = sel.shape[1]

        @pl.loop(0, tiles)
        def _(t):
            for n in range(picks):
                block = sel[t, n]
                put(sel_k, sel_v, n * SEL_BLOCK, kh[block], v[block], kl[block])
            o = attend(rows_of(t), sel_k[...], sel_v[...], None)

            def emit(h, at, x):
                to = pl.ds(pl.multiple_of(t * tile, tile), tile)
                out[to, h * vw : (h + 1) * vw] = (acc[at, :] + x).astype(out.dtype)

            gated(1, t, o, emit)

    relay(1, 1)
    relay(1, 0)
    spread_tokens()
    pass_weights()
    compress()
    for d in range(2, chips - 1):
        relay(d, 1)
        relay(d, 0)
    compressed()
    relay(chips - 1, 1)
    window()
    relay(chips - 1, 0)

    for zz in range(chips):
        slot = zz * CORES + 1 - core
        recv_side(slot, 0)
        early = slot == me - 1
        if zz == chips - 1:
            early = early | (core == 0)

        @pl.when(jnp.logical_not(early))
        def _():
            recv_side(slot, 1)

    selected()

    for d in range(1, n_kv):
        for part in range(2):
            w_msg(d, part).wait_send()
            w_arrived(lax.rem(group + n_kv - d, n_kv), core, part).wait_send()
    for d in range(0, chips):
        comp_send_own(d).wait_send()
    for d in range(1, chips):
        comp_pass(d).wait_send()

    def all_sent(slot, ways):
        for way in ways:
            for half in range(PIECES):
                sent(old_msg, slot, way, half)

    @pl.when(z < chips - 1)
    def _():
        sent(new_msg, me, 1, 0)
        all_sent(me, (1,))

    @pl.when(z > 0)
    def _():
        all_sent(me, (0,))

    sent(new_msg, me, 2, 0)
    all_sent(me, (2,))
    for d in range(1, chips):

        @pl.when(z >= d)
        def _():
            slot = me - CORES * d
            if d <= hops:
                sent(new_msg, slot, 2, 0)

                if d < hops:

                    @pl.when(z < chips - 1)
                    def _():
                        sent(new_msg, slot, 1, 0)

            all_sent(slot, (2,))

            @pl.when(z < chips - 1)
            def _():
                all_sent(slot, (1,))

        @pl.when(z + d < chips)
        def _():
            slot = me + CORES * d
            all_sent(slot, (2,))

            @pl.when(z > 0)
            def _():
                all_sent(slot, (0,))


def shards_gathered(q, ck, cv, ik, iv, wk, wv, sel, gw):
    n_seq, n_kv = lax.axis_size("seq"), lax.axis_size("kv")
    heads, width, branches = gw.shape
    vw = cv.shape[1]
    cache, fresh = ck.shape[0], ik.shape[0]
    tiles, picks = sel.shape[0], sel.shape[-1]
    chunks = cache // CMP_STRIDE
    pad = chunks + CMP_STRIDE
    per, new_per = cache // SEL_BLOCK, fresh // SEL_BLOCK
    tile_rows = heads * fresh
    bf = jnp.bfloat16
    any_spec = pl.BlockSpec(memory_space=pl.ANY)
    half_k, half_v = wk.shape[0] // CORES, wv.shape[0] // CORES

    def held(*shape):
        return pltpu.VMEM(shape, bf)

    dma = pltpu.SemaphoreType.DMA
    return pl.pallas_call(
        functools.partial(fused_kernel, n_seq, n_kv, tiles),
        out_shape=jax.ShapeDtypeStruct((fresh, heads * vw), bf),
        in_specs=[pl.BlockSpec(memory_space=pltpu.SMEM)] + [any_spec] * 8,
        out_specs=pl.BlockSpec(memory_space=pltpu.VMEM),
        scratch_shapes=[
            held(*q.shape),
            held(width, cache),
            held(width, fresh),
            held(heads * branches, width),
            held(n_seq * per, SEL_BLOCK, vw),
            held(n_seq * per, SEL_BLOCK, vw),
            held(n_seq * per, SEL_BLOCK // 2, vw),
            held(n_seq * new_per, SEL_BLOCK, vw),
            held(n_seq * new_per, SEL_BLOCK, vw),
            held(n_seq * new_per, SEL_BLOCK // 2, vw),
            held(cache + CMP_STRIDE, width),
            held(cache + CMP_STRIDE, vw),
            held(CMP_STRIDE * pad, cache + CMP_STRIDE),
            held(pad, CMP_STRIDE * width),
            held(pad, CMP_STRIDE * vw),
            held(n_kv, CORES, width, half_k),
            held(n_kv, CORES, half_v, vw),
            held(2 * chunks + chunks // 2, vw),
            held(n_seq, 2 * chunks + chunks // 2, vw),
            held(n_seq * chunks, width),
            held(n_seq * chunks, vw),
            held(tile_rows, width),
            pltpu.VMEM((tile_rows, heads * branches), jnp.float32),
            pltpu.VMEM((tile_rows, vw), jnp.float32),
            held(fresh + WINDOW, width),
            held(fresh + WINDOW, vw),
            held(picks * SEL_BLOCK, width),
            held(picks * SEL_BLOCK, vw),
            dma((6 + 2 * CORES,)),
            dma,
            dma((3, n_seq, 3, PIECES)),
            dma((n_seq, 3, PIECES)),
            dma((3, n_seq, 3)),
            dma((n_seq, 3)),
            dma((2 * (n_kv - 1), 2)),
            dma((n_kv, CORES, 2)),
            dma((n_seq - 1,)),
            dma((n_seq,)),
        ],
        compiler_params=pltpu.CompilerParams(
            collective_id=0, has_side_effects=True, vmem_limit_bytes=60 << 20
        ),
    )(
        sel.reshape(tiles, picks),
        q,
        ck.T,
        cv.reshape(per, SEL_BLOCK, vw),
        ik.T,
        iv.reshape(new_per, SEL_BLOCK, vw),
        wk.T,
        wv,
        jnp.transpose(gw, (2, 0, 1)).reshape(heads * branches, width),
    )


GATHER_BYTES = 1 << 24


def shards(queries, cache_keys, cache_values, *rest):
    ranks = lax.axis_size("seq")
    size = ranks * 2 * (cache_keys.size + cache_values.size)
    form = shards_gathered if size <= GATHER_BYTES else shards_by_request
    return form(queries, cache_keys, cache_values, *rest)


def solution(mesh):
    placed = (
        P("seq", "kv"),
        P("seq", "kv"),
        P("seq", "kv"),
        P("seq", "kv"),
        P("seq", "kv"),
        P("kv", None),
        P("kv", None),
        P("seq", "kv", None),
        P("kv", None, None),
    )
    return jax.shard_map(
        shards, mesh=mesh, in_specs=placed, out_specs=P("seq", "kv"), check_vma=False
    )
```
